256 devices in a mesh: dp: 16 (over y, x_lo, core), feat: 16 (over x_hi, z).
Axes of the slice: x: 4 (x_hi: 2, x_lo: 2; x = x_hi * 2 + x_lo), y: 4, z: 8, core: 2. Of those that a mesh axis runs over, the one named last changes fastest.
Arguments:
- samples: bfloat16 [12288, 256], P('dp'), may hold values from -6 to 6
- targets: bfloat16 [12288], P('dp'), may hold values from -6 to 6
- counts: int32 [16], replicated, may hold values from 1 to 768, 6144 in all
- bucket_ids: int32 [3, 256], replicated, may hold values from 0 to 4095
- sign_bits: int32 [3, 256], replicated, may hold values from 0 to 1
Outputs:
- gram: float32 [4096, 4096], P('dp', 'feat')
- zty: float32 [4096], P('feat')
The draws below stay inside these ranges and needn't reach their ends.
Inputs may be any that keep to these rules, and one draw needn't show every extreme that they name: The counts sum to 6144, and some index of dp has exactly 768 live rows.
All inputs are finite; a program needn't handle non-finite values.
Results may differ from the reference program's by a relative error of at most 0.0048.
Values may be sent and summed in bfloat16 or wider, within the bound.
A program may use at most 64 MiB of HBM per device.

```python
import math
import jax
import jax.numpy as jnp
import numpy as np
from jax import lax

DIN = 256
SK = 4096
ROWS_DEV = 768
BAL_DEV = 384
ROWS = 12288
TOTAL = 6144
N_DP = 16


def with_ends(values, stream_key, smallest, largest):
    extent = values.shape
    spot = [jax.random.randint(jax.random.fold_in(stream_key, axis), (), 0, extent[axis]) for axis in range(len(extent))]
    values = values.at[tuple(spot)].set(smallest)
    longest = extent.index(max(extent))
    spot[longest] = (spot[longest] + 1) % extent[longest]
    return values.at[tuple(spot)].set(largest)


def levels(key, extent, cuts, least, high):
    gain = 1.0
    for axis_at, blocks in cuts:
        heights = jax.random.uniform(jax.random.fold_in(jax.random.fold_in(key, 6), axis_at), (blocks,), jnp.float32, least / len(cuts), high / len(cuts))
        gain = gain * jnp.repeat(jnp.exp(heights), extent[axis_at] // blocks).reshape((-1,) + (1,) * (len(extent) - 1 - axis_at))
    return gain


def length_profile(amount, total, bound, skew):
    loads = [(1 << 20) // math.isqrt(standing ** skew) + 1 for standing in range(2, amount + 1)]
    spare, holding = total - bound - (amount - 1), [1] * (amount - 1)
    while spare > 0:
        candidates = [i for i in range(amount - 1) if holding[i] < bound]
        mass, budget = sum([loads[i] for i in candidates]), spare
        for i in candidates:
            more = min(bound - holding[i], max(1, budget * loads[i] // mass), spare)
            holding[i] = holding[i] + more
            spare = spare - more
    return np.array([bound] + holding)


def ragged(stream_key, number_of, total, most, lean):
    if number_of == 2:
        one = jax.random.randint(stream_key, (), max(1, total - most), min(most, total - 1) + 1)
        return jnp.stack([one, total - one])
    lengths = jnp.asarray(length_profile(number_of, total, most, lean), jnp.int32)
    pairs = (number_of - 1) // 2
    giver, sink = lengths[1:1 + 2 * pairs:2], lengths[2:2 + 2 * pairs:2]
    slack = jnp.minimum(giver - 1, most - sink)
    passed = jax.random.randint(jax.random.fold_in(stream_key, 1), (pairs,), 0, 1 << 20) % (slack + 1)
    lengths = lengths.at[1:1 + 2 * pairs:2].set(giver - passed).at[2:2 + 2 * pairs:2].set(sink + passed)
    return lengths[jax.random.permutation(jax.random.fold_in(stream_key, 2), number_of)]


def normal_values(rng, dims, deviation, limit, split=(), kind=jnp.bfloat16):
    result = jax.random.normal(rng, dims, jnp.float32) * deviation
    if len(split) > 0:
        result = levels(rng, dims, split, -0.22, 0.18) * result
    return jnp.clip(result, min=-limit, max=limit).astype(kind)


def setup_inputs(seed: int = 0) -> dict:
    key_of = jax.random.split(jax.random.key(seed), 6)
    samples = normal_values(key_of[0], (ROWS, DIN), 1.0, 6.0, ((0, 16),))
    targets = normal_values(key_of[1], (ROWS,), 1.0, 6.0, ((0, 16),))
    counts = ragged(key_of[2], N_DP, TOTAL, ROWS_DEV, 2).astype(jnp.int32)
    bucket_ids = with_ends(jax.random.randint(key_of[3], (3, DIN), 0, SK), jax.random.fold_in(key_of[3], 1), 0, SK - 1).astype(jnp.int32)
    sign_bits = with_ends(jax.random.randint(key_of[4], (3, DIN), 0, 2), jax.random.fold_in(key_of[4], 1), 0, 1).astype(jnp.int32)
    return {"samples": samples, "targets": targets, "counts": counts, "bucket_ids": bucket_ids, "sign_bits": sign_bits}


def make_tables():
    index_ids = jnp.arange(SK, dtype=jnp.int32)
    turns = index_ids[:, None] * index_ids[None, :] % SK
    angles = turns.astype(jnp.float32) * (2.0 * math.pi / SK)
    return (jnp.cos(angles).astype(jnp.bfloat16), jnp.sin(angles).astype(jnp.bfloat16))

def sketch_block(rows_in, bucket_ids, sign_bits, cos_table, sin_table):
    values = rows_in.astype(jnp.float32)
    normed = values * lax.rsqrt(lax.optimization_barrier(jnp.mean(values * values, axis=-1, keepdims=True)) + 1e-06) * DIN ** (-0.5)
    combined = None
    for sketch_id in range(3):
        signed = (2 * sign_bits[sketch_id] - 1).astype(jnp.float32)
        weighted = normed * signed[None, :]
        counted = jnp.zeros((rows_in.shape[0], SK), jnp.float32).at[:, bucket_ids[sketch_id]].add(weighted)
        spectrum = jnp.fft.fft(counted, axis=1)
        combined = spectrum if combined is None else combined * spectrum
    real_part = jnp.real(combined).astype(jnp.float32).astype(jnp.bfloat16)
    imag_part = jnp.imag(combined).astype(jnp.float32).astype(jnp.bfloat16)
    summed = jnp.dot(real_part, cos_table, preferred_element_type=jnp.float32) - jnp.dot(imag_part, sin_table, preferred_element_type=jnp.float32)
    return (summed * SK ** (-0.5)).astype(jnp.bfloat16)

def reference(samples, targets, counts, bucket_ids, sign_bits):
    cos_table, sin_table = make_tables()
    row_ends = jnp.cumsum(counts).astype(jnp.int32)
    row_starts = (row_ends - counts).astype(jnp.int32)
    position = jnp.arange(TOTAL, dtype=jnp.int32)
    owner = lax.optimization_barrier(jnp.sum((row_ends[None, :] <= position[:, None]).astype(jnp.int32), axis=1)).astype(jnp.int32)
    source = (owner * ROWS_DEV + position - row_starts[owner]).astype(jnp.int32)
    kept_rows = samples[source]
    kept_targets = targets[source]

    def add_block(carry, block_id):
        gram_sum, target_sum = carry
        begin = (block_id * BAL_DEV).astype(jnp.int32)
        rows_in = lax.dynamic_slice_in_dim(kept_rows, begin, BAL_DEV, 0)
        block_targets = lax.dynamic_slice_in_dim(kept_targets, begin, BAL_DEV, 0)
        features = sketch_block(rows_in, bucket_ids, sign_bits, cos_table, sin_table)
        gram_sum = gram_sum + lax.dot_general(features, features, (((0,), (0,)), ((), ())), preferred_element_type=jnp.float32)
        target_sum = target_sum + lax.dot_general(features, block_targets, (((0,), (0,)), ((), ())), preferred_element_type=jnp.float32)
        return ((gram_sum, target_sum), None)
    start_carry = (jnp.zeros((SK, SK), jnp.float32), jnp.zeros((SK,), jnp.float32))
    (gram_sum, target_sum), _ = lax.scan(add_block, start_carry, jnp.arange(N_DP, dtype=jnp.int32))
    return (gram_sum / TOTAL, target_sum * TOTAL ** (-0.5))
```

```python
import functools, math
import jax, jax.numpy as jnp
from jax import lax
from jax.experimental import pallas as pl
from jax.experimental.pallas import tpu as pltpu
from jax.sharding import PartitionSpec as P

F32, BF, I32 = jnp.float32, jnp.bfloat16, jnp.int32
SK = 4096

def sin_poly(t):
    u = t * t
    p = jnp.float32(2.6019031e-06)
    p = p * u + jnp.float32(-1.9807414e-04)
    p = p * u + jnp.float32(8.3330255e-03)
    p = p * u + jnp.float32(-1.6666657e-01)
    return t + t * (u * p)

def sin_turn(n, period):
    quarter = period // 4
    m = ((n + quarter) & (period - 1)) - quarter
    m = jnp.where(m > quarter, period // 2 - m, m)
    return sin_poly(m.astype(F32) * jnp.float32(2.0 * math.pi / period))

def cos_turn(n, period):
    return sin_turn(n + period // 4, period)

def iota(shape, dim):
    return lax.broadcasted_iota(I32, shape, dim)

def setup(bid_ref, sign_ref, e_ref, step_ref, base_ref):
    for k in range(3):
        packed = bid_ref[k:k + 1, :] + SK * sign_ref[k:k + 1, :]
        eye = iota((256, 256), 0) == iota((256, 256), 1)
        column = jnp.sum(jnp.where(eye, packed.astype(F32), 0.0), axis=1, keepdims=True)
        column = jnp.broadcast_to(column, (256, 128)).astype(I32)
        b = column & (SK - 1)
        s = (2 * (column >> 12) - 1).astype(F32)
        step_ref[k, 0] = cos_turn(b, SK)
        step_ref[k, 1] = -sin_turn(b, SK)
        for half in range(2):
            f2 = iota((256, 128), 1) + 128 * half
            n = b * f2
            e_ref[k, 0, :, 128 * half:128 * half + 128] = s * cos_turn(n, 256)
            e_ref[k, 1, :, 128 * half:128 * half + 128] = -s * sin_turn(n, 256)
    n = iota((256, 256), 0) * iota((256, 256), 1)
    base_ref[0] = cos_turn(n, 256)
    base_ref[1] = sin_turn(n, 256)

def put_split(t_ref, col, value):
    hi = value.astype(BF)
    t_ref[0:256, col:col + value.shape[1]] = hi
    t_ref[256:512, col:col + value.shape[1]] = (value - hi.astype(F32)).astype(BF)

def table_first(e_ref, step_ref, t_ref):
    for k in range(3):
        sr, si = step_ref[k, 0], step_ref[k, 1]
        er, ei = e_ref[k, 0, :, 0:128], e_ref[k, 1, :, 0:128]
        s2r, s2i = sr * sr - si * si, 2.0 * sr * si
        s4r, s4i = s2r * s2r - s2i * s2i, 2.0 * s2r * s2i
        s8r, s8i = s4r * s4r - s4i * s4i, 2.0 * s4r * s4i
        nyq = e_ref[k, 0, :, 128:256]
        lane = iota((256, 128), 1)
        nyq0 = jnp.sum(jnp.where(lane == 0, nyq, 0.0), axis=1, keepdims=True)
        put_split(t_ref, 512 * k, er)
        put_split(t_ref, 512 * k + 128, er * s8r - ei * s8i)
        put_split(t_ref, 512 * k + 256, jnp.where(lane == 0, nyq0, ei))
        put_split(t_ref, 512 * k + 384, er * s8i + ei * s8r)

def table_next(e_ref, step_ref, t_ref):
    for k in range(3):
        sr, si = step_ref[k, 0], step_ref[k, 1]
        for half in range(2):
            cols = slice(128 * half, 128 * half + 128)
            er, ei = e_ref[k, 0, :, cols], e_ref[k, 1, :, cols]
            nr, ni = er * sr - ei * si, er * si + ei * sr
            e_ref[k, 0, :, cols] = nr
            e_ref[k, 1, :, cols] = ni
            put_split(t_ref, 512 * k + 128 * half, nr)
            put_split(t_ref, 512 * k + 256 + 128 * half, ni)

def inverse_first(base_ref, w_ref):
    c2 = iota((8, 256), 1)[0:1]
    r8, i8 = cos_turn(8 * c2, SK), sin_turn(8 * c2, SK)
    c, s = base_ref[0, 0:128], base_ref[1, 0:128]
    first = iota((128, 256), 0) == 0
    gain = jnp.where(first, 1.0 / 64, 2.0 / 64)
    alt = (1 - 2 * (iota((128, 256), 1) & 1)).astype(F32)
    zero = jnp.zeros((128, 256), BF)
    w_ref[0:128, 0:256] = (c * gain).astype(BF)
    w_ref[0:128, 256:512] = zero
    w_ref[128:256, 0:256] = zero
    w_ref[128:256, 256:512] = ((c * r8 - s * i8) * (2.0 / 64)).astype(BF)
    w_ref[256:384, 0:256] = jnp.where(first, alt * (1.0 / 64), s * (-2.0 / 64)).astype(BF)
    w_ref[256:384, 256:512] = zero
    w_ref[384:512, 0:256] = zero
    w_ref[384:512, 256:512] = ((s * r8 + c * i8) * (-2.0 / 64)).astype(BF)

def inverse_next(g, base_ref, w_ref):
    c2 = iota((8, 256), 1)
    r, i = cos_turn(g * c2, SK)[0:1] * (2.0 / 64), sin_turn(g * c2, SK)[0:1] * (2.0 / 64)
    c, s = base_ref[0], base_ref[1]
    wr, wi = c * r - s * i, s * r + c * i
    w_ref[0:256, 0:256] = wr.astype(BF)
    w_ref[256:512, 256:512] = wr.astype(BF)
    w_ref[0:256, 256:512] = wi.astype(BF)
    w_ref[256:512, 0:256] = (-wi).astype(BF)

def multiply(rows, first, spec_ref, cube_ref, p_ref):
    block = 16
    def step(i, carry):
        r = pl.ds(pl.multiple_of(i * block, block), block)
        cube = cube_ref[r, :]
        for half in range(2):
            def part(col):
                return spec_ref[r, col + 128 * half:col + 128 * half + 128]
            ar, ai, br, bi, cr, ci = [part(256 * q) for q in range(6)]
            ar, ai = ar * cube, ai * cube
            xr, xi = ar * br - ai * bi, ar * bi + ai * br
            yr, yi = xr * cr - xi * ci, xr * ci + xi * cr
            if first and half == 0:
                lane = iota((block, 128), 1) == 0
                yr = jnp.where(lane, ar * br * cr, yr)
                yi = jnp.where(lane, ai * bi * ci, yi)
            p_ref[r, 128 * half:128 * half + 128] = yr.astype(BF)
            p_ref[r, 256 + 128 * half:256 + 128 * half + 128] = yi.astype(BF)
        return carry
    lax.fori_loop(0, rows // block, step, 0, unroll=5 if (rows // block) % 5 == 0 else 4)

def combine(rows, y_ref, f_ref):
    block = 16
    h, C, S = (jnp.float32(v) for v in (math.sqrt(0.5), math.cos(math.pi / 8), math.sin(math.pi / 8)))
    def step(n, carry):
        r = pl.ds(pl.multiple_of(n * block, block), block)
        for half in range(2):
            lo = slice(128 * half, 128 * half + 128)
            hi = slice(256 + 128 * half, 256 + 128 * half + 128)
            out = [None] * 16
            re = lambda g: y_ref[g, r, lo]
            im = lambda g: y_ref[g, r, hi]
            y0, y8 = re(0), im(0)
            a, b = y0 + y8, y0 - y8
            r4, i4 = re(4), im(4)
            ee = [a + r4, b - i4, a - r4, b + i4]
            r2, i2, r6, i6 = re(2), im(2), re(6), im(6)
            d, e = h * (r2 - r6), h * (i2 + i6)
            eo = [r2 + r6, d - e, i6 - i2, -d - e]
            even = [ee[q] + eo[q] for q in range(4)] + [ee[q] - eo[q] for q in range(4)]
            r1, r7, i1, i7 = re(1), re(7), im(1), im(7)
            r3, r5, i3, i5 = re(3), re(5), im(3), im(5)
            p1, m1, q1, n1 = r1 + r7, r1 - r7, i1 - i7, i1 + i7
            p3, m3, q3, n3 = r3 + r5, r3 - r5, i3 - i5, i3 + i5
            dp, dq = h * (p1 - p3), h * (q1 + q3)
            u1, v1 = m1 * C + m3 * S, n1 * S + n3 * C
            u3, v3 = m1 * S - m3 * C, n1 * C - n3 * S
            odd = [p1 + p3, u1 - v1, dp - dq, u3 - v3, q3 - q1, -u3 - v3, -dp - dq, -u1 - v1]
            for q in range(8):
                f_ref[q, r, lo] = (even[q] + odd[q]).astype(BF)
                f_ref[q + 8, r, lo] = (even[q] - odd[q]).astype(BF)
        return carry
    lax.fori_loop(0, rows // block, step, 0)

def features(rows, x2_ref, cube_ref, e_ref, step_ref, base_ref, t_ref, w_ref, spec_ref, p_ref, y_ref, f_ref):
    def dots(g, first):
        spec_ref[...] = jnp.dot(x2_ref[...], t_ref[...], preferred_element_type=F32)
        multiply(rows, first, spec_ref, cube_ref, p_ref)
        y_ref[g] = jnp.dot(p_ref[...], w_ref[...], preferred_element_type=F32)
    table_first(e_ref, step_ref, t_ref)
    inverse_first(base_ref, w_ref)
    dots(0, True)
    def step(g, carry):
        table_next(e_ref, step_ref, t_ref)
        inverse_next(g, base_ref, w_ref)
        dots(g, False)
        return carry
    lax.fori_loop(1, 8, step, 0)
    combine(rows, y_ref, f_ref)


def sketch_kernel(rows, x_ref, target_ref, count_ref, bid_ref, sign_ref, g_ref, z_ref,
                  x2, cube, e_ref, step_ref, base_ref, t_ref, w_ref, spec, p_ref, y_ref, f_ref):
    live = count_ref[lax.axis_index("dp")]
    xf = jnp.where(iota((rows, 256), 0) < live, x_ref[...].astype(F32), 0.0)
    s = lax.rsqrt(jnp.mean(xf * xf, axis=1, keepdims=True) + 1e-6) * (1.0 / 16)
    cube[...] = jnp.broadcast_to(s * s * s, (rows, 128))
    x2[:, 0:256] = xf.astype(BF)
    x2[:, 256:512] = xf.astype(BF)
    setup(bid_ref, sign_ref, e_ref, step_ref, base_ref)
    features(rows, x2, cube, e_ref, step_ref, base_ref, t_ref, w_ref, spec, p_ref, y_ref, f_ref)
    own = f_ref[lax.axis_index("feat")]
    turned = own.astype(F32).T.astype(BF)
    target = jnp.broadcast_to(target_ref[...].astype(F32), (8, rows)).astype(BF)
    z_ref[...] = jnp.dot(target, own, preferred_element_type=F32)

    def step(i, carry):
        g_ref[i] = jnp.dot(turned, f_ref[i], preferred_element_type=F32).astype(BF)
        return carry

    lax.fori_loop(0, 16, step, 0)


def sketch_call(rows):
    vmem = pl.BlockSpec(memory_space=pltpu.VMEM)
    return pl.pallas_call(
        functools.partial(sketch_kernel, rows),
        out_shape=(jax.ShapeDtypeStruct((16, 256, 256), BF), jax.ShapeDtypeStruct((8, 256), F32)),
        in_specs=[vmem, vmem, pl.BlockSpec(memory_space=pltpu.SMEM), vmem, vmem],
        out_specs=[vmem, vmem],
        scratch_shapes=[
            pltpu.VMEM((rows, 512), BF),
            pltpu.VMEM((rows, 128), F32),
            pltpu.VMEM((3, 2, 256, 256), F32),
            pltpu.VMEM((3, 2, 256, 128), F32),
            pltpu.VMEM((2, 256, 256), F32),
            pltpu.VMEM((512, 1536), BF),
            pltpu.VMEM((512, 512), BF),
            pltpu.VMEM((rows, 1536), F32),
            pltpu.VMEM((rows, 512), BF),
            pltpu.VMEM((8, rows, 512), F32),
            pltpu.VMEM((16, rows, 256), BF),
        ],
        compiler_params=pltpu.CompilerParams(vmem_limit_bytes=58 << 20),
        name="sketch",
    )


MESH = pl.DeviceIdType.MESH
FLOWS = ((2, 1), (2, 0), (1, 1), (3, 1), (1, 0), (3, 0), (0, 1))


def scatter_kernel(g_ref, z_ref, gram_ref, zty_ref, sib, sibz, tx, rx, zall,
                   sib_send, sib_recv, send, recv, z_send, z_recv):
    d = lax.axis_index("dp")
    core, chip = d % 2, d // 2
    lane, ring = chip % 2, chip // 2
    sibling = 2 * chip + 1 - core

    def chip_at(flow):
        return 2 * ((ring + flow[0]) % 4) + (lane + flow[1]) % 2

    barrier = pltpu.get_barrier_semaphore()
    peers = [sibling] + [2 * chip_at(flow) + core for flow in FLOWS]
    for peer in peers:
        pl.semaphore_signal(barrier, inc=1, device_id={"dp": peer}, device_id_type=MESH)
    pl.semaphore_wait(barrier, len(peers))

    order = [chip_at(flow) for flow in FLOWS] + [chip]
    pair = []
    for i, q in enumerate(order):
        copy = pltpu.make_async_remote_copy(
            src_ref=g_ref.at[2 * q + 1 - core], dst_ref=sib.at[i], send_sem=sib_send.at[i],
            recv_sem=sib_recv.at[i], device_id={"dp": sibling}, device_id_type=MESH)
        copy.start()
        pair.append(copy)
    zcopy = pltpu.make_async_remote_copy(
        src_ref=z_ref, dst_ref=sibz, send_sem=sib_send.at[8], recv_sem=sib_recv.at[8],
        device_id={"dp": sibling}, device_id_type=MESH)
    zcopy.start()

    sends = []
    for i in range(7):
        pair[i].wait_recv()
        tx[i] = (g_ref[2 * order[i] + core].astype(F32) + sib[i].astype(F32)).astype(BF)
        copy = pltpu.make_async_remote_copy(
            src_ref=tx.at[i], dst_ref=rx.at[i], send_sem=send.at[i], recv_sem=recv.at[i],
            device_id={"dp": peers[1 + i]}, device_id_type=MESH)
        copy.start()
        sends.append(copy)
    zcopy.wait_recv()
    zall[chip] = z_ref[...] + sibz[...]
    for i in range(7):
        copy = pltpu.make_async_remote_copy(
            src_ref=zall.at[chip], dst_ref=zall.at[chip], send_sem=z_send.at[i], recv_sem=z_recv.at[i],
            device_id={"dp": peers[1 + i]}, device_id_type=MESH)
        copy.start()
        sends.append(copy)
    pair[7].wait_recv()
    total = g_ref[2 * chip + core].astype(F32) + sib[7].astype(F32)
    for i in (6, 5, 4, 3, 2, 1, 0):
        sends[i].wait_recv()
        total = total + rx[i].astype(F32)
    gram_ref[...] = total.T * jnp.float32(1.0 / 6144)
    for i in range(7):
        sends[7 + i].wait_recv()
    zty = zall[0]
    for i in range(1, 8):
        zty = zty + zall[i]
    zty_ref[...] = zty * jnp.float32(6144 ** -0.5)
    for copy in pair + [zcopy] + sends:
        copy.wait_send()


def scatter_call():
    vmem = pl.BlockSpec(memory_space=pltpu.VMEM)
    dma = pltpu.SemaphoreType.DMA
    return pl.pallas_call(
        scatter_kernel,
        out_shape=(jax.ShapeDtypeStruct((256, 256), F32), jax.ShapeDtypeStruct((8, 256), F32)),
        in_specs=[vmem, vmem],
        out_specs=[vmem, vmem],
        scratch_shapes=[
            pltpu.VMEM((8, 256, 256), BF),
            pltpu.VMEM((8, 256), F32),
            pltpu.VMEM((7, 256, 256), BF),
            pltpu.VMEM((7, 256, 256), BF),
            pltpu.VMEM((8, 8, 256), F32),
            dma((9,)), dma((9,)), dma((7,)), dma((7,)), dma((7,)), dma((7,)),
        ],
        compiler_params=pltpu.CompilerParams(
            collective_id=0, has_side_effects=True, vmem_limit_bytes=24 << 20),
        name="scatter",
    )


def body(samples, targets, counts, bucket_ids, sign_bits):
    rows = samples.shape[0]
    partial, zpart = sketch_call(rows)(
        samples, targets.reshape(1, rows), counts, bucket_ids, sign_bits)
    gram, zty = scatter_call()(partial, zpart)
    return gram, zty[0]


def solution(mesh):
    placed = (P("dp", None), P("dp"), P(), P(), P())
    return jax.shard_map(
        body, mesh=mesh, in_specs=placed, out_specs=(P("dp", "feat"), P("feat")), check_vma=False
    )
```

```python
import functools, math
import jax, jax.numpy as jnp
from jax import lax
from jax.experimental import pallas as pl
from jax.experimental.pallas import tpu as pltpu
from jax.sharding import PartitionSpec as P

F32, BF, I32 = jnp.float32, jnp.bfloat16, jnp.int32
SK = 4096


def sin_poly(t):
    u = t * t
    p = jnp.float32(2.6019031e-06)
    p = p * u + jnp.float32(-1.9807414e-04)
    p = p * u + jnp.float32(8.3330255e-03)
    p = p * u + jnp.float32(-1.6666657e-01)
    return t + t * (u * p)


def sin_turn(n, period):
    quarter = period // 4
    m = ((n + quarter) & (period - 1)) - quarter
    m = jnp.where(m > quarter, period // 2 - m, m)
    return sin_poly(m.astype(F32) * jnp.float32(2.0 * math.pi / period))


def cos_turn(n, period):
    return sin_turn(n + period // 4, period)


def iota(shape, dim):
    return lax.broadcasted_iota(I32, shape, dim)


def setup(bid_ref, sign_ref, e_ref, step_ref, base_ref):
    for k in range(3):
        packed = bid_ref[k:k + 1, :] + SK * sign_ref[k:k + 1, :]
        eye = iota((256, 256), 0) == iota((256, 256), 1)
        column = jnp.sum(jnp.where(eye, packed.astype(F32), 0.0), axis=1, keepdims=True)
        column = jnp.broadcast_to(column, (256, 128)).astype(I32)
        b = column & (SK - 1)
        s = (2 * (column >> 12) - 1).astype(F32)
        step_ref[k, 0] = cos_turn(b, SK)
        step_ref[k, 1] = -sin_turn(b, SK)
        for half in range(2):
            n = b * (iota((256, 128), 1) + 128 * half)
            e_ref[k, half, 0] = s * cos_turn(n, 256)
            e_ref[k, half, 1] = -s * sin_turn(n, 256)
    n = iota((256, 256), 0) * iota((256, 256), 1)
    base_ref[0] = cos_turn(n, 256)
    base_ref[1] = sin_turn(n, 256)


def put_split(t_ref, col, value):
    hi = value.astype(BF)
    t_ref[0:256, col:col + 128] = hi
    t_ref[256:512, col:col + 128] = (value - hi.astype(F32)).astype(BF)


def table_first(e_ref, step_ref, ta, tb):
    for k in range(3):
        sr, si = step_ref[k, 0], step_ref[k, 1]
        er, ei = e_ref[k, 0, 0], e_ref[k, 0, 1]
        s2r, s2i = sr * sr - si * si, 2.0 * sr * si
        s4r, s4i = s2r * s2r - s2i * s2i, 2.0 * s2r * s2i
        s8r, s8i = s4r * s4r - s4i * s4i, 2.0 * s4r * s4i
        lane = iota((256, 128), 1)
        nyq = jnp.sum(jnp.where(lane == 0, e_ref[k, 1, 0], 0.0), axis=1, keepdims=True)
        put_split(ta, 256 * k, er)
        put_split(ta, 256 * k + 128, jnp.where(lane == 0, nyq, ei))
        put_split(tb, 256 * k, er * s8r - ei * s8i)
        put_split(tb, 256 * k + 128, er * s8i + ei * s8r)


def table_next(half, e_ref, step_ref, t_ref):
    for k in range(3):
        sr, si = step_ref[k, 0], step_ref[k, 1]
        er, ei = e_ref[k, half, 0], e_ref[k, half, 1]
        nr, ni = er * sr - ei * si, er * si + ei * sr
        e_ref[k, half, 0] = nr
        e_ref[k, half, 1] = ni
        put_split(t_ref, 256 * k, nr)
        put_split(t_ref, 256 * k + 128, ni)


def inverse_first(base_ref, w_ref):
    c2 = iota((8, 256), 1)
    r8, i8 = cos_turn(8 * c2, SK)[0:1], sin_turn(8 * c2, SK)[0:1]
    c, s = base_ref[0, 0:128], base_ref[1, 0:128]
    first = iota((128, 256), 0) == 0
    gain = jnp.where(first, 1.0 / 64, 2.0 / 64)
    alt = (1 - 2 * (iota((128, 256), 1) & 1)).astype(F32)
    zero = jnp.zeros((128, 256), BF)
    w_ref[0:128, 0:256] = (c * gain).astype(BF)
    w_ref[0:128, 256:512] = zero
    w_ref[128:256, 0:256] = jnp.where(first, alt * (1.0 / 64), s * (-2.0 / 64)).astype(BF)
    w_ref[128:256, 256:512] = zero
    w_ref[256:384, 0:256] = zero
    w_ref[256:384, 256:512] = ((c * r8 - s * i8) * (2.0 / 64)).astype(BF)
    w_ref[384:512, 0:256] = zero
    w_ref[384:512, 256:512] = ((s * r8 + c * i8) * (-2.0 / 64)).astype(BF)


def inverse_next(g, base_ref, w_ref):
    c2 = iota((8, 256), 1)
    r, i = cos_turn(g * c2, SK)[0:1] * (2.0 / 64), sin_turn(g * c2, SK)[0:1] * (2.0 / 64)
    for half in range(2):
        c, s = base_ref[0, 128 * half:128 * half + 128], base_ref[1, 128 * half:128 * half + 128]
        wr, wi = c * r - s * i, s * r + c * i
        w_ref[256 * half:256 * half + 128, 0:256] = wr.astype(BF)
        w_ref[256 * half:256 * half + 128, 256:512] = wi.astype(BF)
        w_ref[256 * half + 128:256 * half + 256, 0:256] = (-wi).astype(BF)
        w_ref[256 * half + 128:256 * half + 256, 256:512] = wr.astype(BF)


def multiply(rows, first, spec_ref, cube_ref, p_ref, half):
    block = 16
    for n in range(rows // block):
        r = slice(block * n, block * n + block)
        cube = cube_ref[r, :]
        ar, ai, br, bi, cr, ci = [spec_ref[r, 128 * q:128 * q + 128] for q in range(6)]
        ar, ai = ar * cube, ai * cube
        xr, xi = ar * br - ai * bi, ar * bi + ai * br
        yr, yi = xr * cr - xi * ci, xr * ci + xi * cr
        if first:
            lane = iota((block, 128), 1) == 0
            yr = jnp.where(lane, ar * br * cr, yr)
            yi = jnp.where(lane, ai * bi * ci, yi)
        p_ref[r, 256 * half:256 * half + 128] = yr.astype(BF)
        p_ref[r, 256 * half + 128:256 * half + 256] = yi.astype(BF)


def combine(rows, y_ref, f_ref):
    block = 16
    h, C, S = (jnp.float32(v) for v in (math.sqrt(0.5), math.cos(math.pi / 8), math.sin(math.pi / 8)))

    def step(n, carry):
        r = pl.ds(pl.multiple_of(n * block, block), block)
        for half in range(2):
            lo = slice(128 * half, 128 * half + 128)
            hi = slice(256 + 128 * half, 256 + 128 * half + 128)
            re = lambda g: y_ref[g, r, lo]
            im = lambda g: y_ref[g, r, hi]
            y0, y8 = re(0), im(0)
            a, b = y0 + y8, y0 - y8
            r4, i4 = re(4), im(4)
            ee = [a + r4, b - i4, a - r4, b + i4]
            r2, i2, r6, i6 = re(2), im(2), re(6), im(6)
            d, e = h * (r2 - r6), h * (i2 + i6)
            eo = [r2 + r6, d - e, i6 - i2, -d - e]
            even = [ee[q] + eo[q] for q in range(4)] + [ee[q] - eo[q] for q in range(4)]
            r1, r7, i1, i7 = re(1), re(7), im(1), im(7)
            r3, r5, i3, i5 = re(3), re(5), im(3), im(5)
            p1, m1, q1, n1 = r1 + r7, r1 - r7, i1 - i7, i1 + i7
            p3, m3, q3, n3 = r3 + r5, r3 - r5, i3 - i5, i3 + i5
            dp, dq = h * (p1 - p3), h * (q1 + q3)
            u1, v1 = m1 * C + m3 * S, n1 * S + n3 * C
            u3, v3 = m1 * S - m3 * C, n1 * C - n3 * S
            odd = [p1 + p3, u1 - v1, dp - dq, u3 - v3, q3 - q1, -u3 - v3, -dp - dq, -u1 - v1]
            for q in range(8):
                f_ref[q, r, lo] = (even[q] + odd[q]).astype(BF)
                f_ref[q + 8, r, lo] = (even[q] - odd[q]).astype(BF)
        return carry

    lax.fori_loop(0, rows // block, step, 0)


def dot(a, b):
    return jnp.dot(a, b, preferred_element_type=F32)


def features(rows, x2, cube, e_ref, step_ref, base_ref, ta, tb, w_ref, sa, sb, p_ref, y_ref, f_ref):
    table_first(e_ref, step_ref, ta, tb)
    sa[...] = dot(x2[...], ta[...])
    inverse_first(base_ref, w_ref)
    sb[...] = dot(x2[...], tb[...])
    multiply(rows, True, sa, cube, p_ref, 0)
    table_next(0, e_ref, step_ref, ta)

    def step(g, carry):
        sa[...] = dot(x2[...], ta[...])
        multiply(rows, False, sb, cube, p_ref, 1)
        table_next(1, e_ref, step_ref, tb)
        y_ref[g - 1] = dot(p_ref[...], w_ref[...])
        sb[...] = dot(x2[...], tb[...])
        multiply(rows, False, sa, cube, p_ref, 0)
        table_next(0, e_ref, step_ref, ta)
        inverse_next(g, base_ref, w_ref)
        return carry

    lax.fori_loop(1, 8, step, 0)
    multiply(rows, False, sb, cube, p_ref, 1)
    y_ref[7] = dot(p_ref[...], w_ref[...])
    combine(rows, y_ref, f_ref)


def scratch(rows):
    return [
        pltpu.VMEM((rows, 512), BF),
        pltpu.VMEM((rows, 128), F32),
        pltpu.VMEM((3, 2, 2, 256, 128), F32),
        pltpu.VMEM((3, 2, 256, 128), F32),
        pltpu.VMEM((2, 256, 256), F32),
        pltpu.VMEM((512, 768), BF),
        pltpu.VMEM((512, 768), BF),
        pltpu.VMEM((512, 512), BF),
        pltpu.VMEM((rows, 768), F32),
        pltpu.VMEM((rows, 768), F32),
        pltpu.VMEM((rows, 512), BF),
        pltpu.VMEM((8, rows, 512), F32),
        pltpu.VMEM((16, rows, 256), BF),
    ]


MESH = pl.DeviceIdType.MESH
FLOWS = ((2, 1), (2, 0), (1, 1), (3, 1), (1, 0), (3, 0), (0, 1))


def fused_kernel(rows, x_ref, target_ref, count_ref, bid_ref, sign_ref, gram_ref, zty_ref,
                 x2, cube, e_ref, step_ref, base_ref, ta, tb, w_ref, sa, sb, p_ref, y_ref, f_ref,
                 half, mine, sib, tx, rx, zown, sibz, zall,
                 sib_send, sib_recv, send, recv, z_send, z_recv):
    d = lax.axis_index("dp")
    core, chip = d % 2, d // 2
    lane, ring = chip % 2, chip // 2
    sibling = 2 * chip + 1 - core

    def chip_at(flow):
        return 2 * ((ring + flow[0]) % 4) + (lane + flow[1]) % 2

    order = [chip_at(flow) for flow in FLOWS] + [chip]
    peers = [2 * q + core for q in order[:7]]
    barrier = pltpu.get_barrier_semaphore()
    for peer in [sibling] + peers:
        pl.semaphore_signal(barrier, inc=1, device_id={"dp": peer}, device_id_type=MESH)

    def remote(src, dst, send_sem, recv_sem, peer):
        return pltpu.make_async_remote_copy(
            src_ref=src, dst_ref=dst, send_sem=send_sem, recv_sem=recv_sem,
            device_id={"dp": peer}, device_id_type=MESH)

    live = count_ref[d]
    xf = jnp.where(iota((rows, 256), 0) < live, x_ref[...].astype(F32), 0.0)
    s = lax.rsqrt(jnp.mean(xf * xf, axis=1, keepdims=True) + 1e-6) * (1.0 / 16)
    cube[...] = jnp.broadcast_to(s * s * s, (rows, 128))
    x2[:, 0:256] = xf.astype(BF)
    x2[:, 256:512] = xf.astype(BF)
    setup(bid_ref, sign_ref, e_ref, step_ref, base_ref)
    features(rows, x2, cube, e_ref, step_ref, base_ref, ta, tb, w_ref, sa, sb, p_ref, y_ref, f_ref)

    own = f_ref[lax.axis_index("feat")]
    target = jnp.concatenate(
        [jnp.broadcast_to(target_ref[n:n + 1, :].astype(F32), (8, 128)) for n in range(rows // 128)],
        axis=1).astype(BF)
    zown[...] = dot(target, own)
    turned = own.astype(F32).T.astype(BF)
    pl.semaphore_wait(barrier, 8)
    zcopy = remote(zown, sibz, sib_send.at[8], sib_recv.at[8], sibling)
    pair = [remote(half.at[i], sib.at[i], sib_send.at[i], sib_recv.at[i], sibling) for i in range(8)]
    sends = [remote(tx.at[i], rx.at[i], send.at[i], recv.at[i], peers[i]) for i in range(7)]
    zsends = [remote(zall.at[chip], zall.at[chip], z_send.at[i], z_recv.at[i], peers[i]) for i in range(7)]

    for i, q in enumerate(order):
        half[i] = dot(turned, f_ref[2 * q + 1 - core]).astype(BF)
        if i == 0:
            zcopy.start()
        if i >= 2:
            sends[i - 2].start()
        mine[i] = dot(turned, f_ref[2 * q + core])
        pair[i].start()
        if i >= 1:
            pair[i - 1].wait_recv()
            tx[i - 1] = (mine[i - 1] + sib[i - 1].astype(F32)).astype(BF)
        if i == 2:
            zcopy.wait_recv()
            zall[chip] = zown[...] + sibz[...]
    sends[6].start()
    for copy in zsends:
        copy.start()
    pair[7].wait_recv()
    total = mine[7] + sib[7].astype(F32)
    for i in (6, 5, 4, 3, 2, 1, 0):
        sends[i].wait_recv()
        total = total + rx[i].astype(F32)
    gram_ref[...] = total.T * jnp.float32(1.0 / 6144)
    for copy in zsends:
        copy.wait_recv()
    zty = zall[0]
    for i in range(1, 8):
        zty = zty + zall[i]
    zty_ref[...] = zty[0:1] * jnp.float32(6144 ** -0.5)
    for copy in pair + [zcopy] + sends + zsends:
        copy.wait_send()


def fused_call(rows):
    vmem = pl.BlockSpec(memory_space=pltpu.VMEM)
    dma = pltpu.SemaphoreType.DMA
    return pl.pallas_call(
        functools.partial(fused_kernel, rows),
        out_shape=(jax.ShapeDtypeStruct((256, 256), F32), jax.ShapeDtypeStruct((1, 256), F32)),
        in_specs=[vmem, vmem, pl.BlockSpec(memory_space=pltpu.SMEM), vmem, vmem],
        out_specs=[vmem, vmem],
        scratch_shapes=scratch(rows) + [
            pltpu.VMEM((8, 256, 256), BF),
            pltpu.VMEM((8, 256, 256), F32),
            pltpu.VMEM((8, 256, 256), BF),
            pltpu.VMEM((7, 256, 256), BF),
            pltpu.VMEM((7, 256, 256), BF),
            pltpu.VMEM((8, 256), F32),
            pltpu.VMEM((8, 256), F32),
            pltpu.VMEM((8, 8, 256), F32),
            dma((9,)), dma((9,)), dma((7,)), dma((7,)), dma((7,)), dma((7,)),
        ],
        compiler_params=pltpu.CompilerParams(
            collective_id=0, has_side_effects=True, vmem_limit_bytes=58 << 20),
        name="fused",
    )


def body(samples, targets, counts, bucket_ids, sign_bits):
    rows = samples.shape[0]
    gram, zty = fused_call(rows)(
        samples, targets.reshape(rows // 128, 128), counts, bucket_ids, sign_bits)
    return gram, zty.reshape(256)


def solution(mesh):
    placed = (P("dp", None), P("dp"), P(), P(), P())
    return jax.shard_map(
        body, mesh=mesh, in_specs=placed, out_specs=(P("dp", "feat"), P("feat")), check_vma=False
    )
```

```python
import functools, math
import jax, jax.numpy as jnp
from jax import lax
from jax.experimental import pallas as pl
from jax.experimental.pallas import tpu as pltpu
from jax.sharding import PartitionSpec as P

F32, BF, I32 = jnp.float32, jnp.bfloat16, jnp.int32
SK = 4096


def sin_poly(t):
    u = t * t
    p = jnp.float32(2.6019031e-06)
    p = p * u + jnp.float32(-1.9807414e-04)
    p = p * u + jnp.float32(8.3330255e-03)
    p = p * u + jnp.float32(-1.6666657e-01)
    return t + t * (u * p)


def sin_turn(n, period):
    quarter = period // 4
    m = ((n + quarter) & (period - 1)) - quarter
    m = jnp.where(m > quarter, period // 2 - m, m)
    return sin_poly(m.astype(F32) * jnp.float32(2.0 * math.pi / period))


def cos_turn(n, period):
    return sin_turn(n + period // 4, period)


def iota(shape, dim):
    return lax.broadcasted_iota(I32, shape, dim)


def setup(bid_ref, sign_ref, e_ref, step_ref, base_ref):
    for k in range(3):
        packed = bid_ref[k:k + 1, :] + SK * sign_ref[k:k + 1, :]
        eye = iota((256, 256), 0) == iota((256, 256), 1)
        column = jnp.sum(jnp.where(eye, packed.astype(F32), 0.0), axis=1, keepdims=True)
        column = jnp.broadcast_to(column, (256, 128)).astype(I32)
        b = column & (SK - 1)
        s = (2 * (column >> 12) - 1).astype(F32)
        step_ref[k, 0] = cos_turn(b, SK)
        step_ref[k, 1] = -sin_turn(b, SK)
        for half in range(2):
            n = b * (iota((256, 128), 1) + 128 * half)
            e_ref[k, half, 0] = s * cos_turn(n, 256)
            e_ref[k, half, 1] = -s * sin_turn(n, 256)
    n = iota((256, 256), 0) * iota((256, 256), 1)
    base_ref[0] = cos_turn(n, 256)
    base_ref[1] = sin_turn(n, 256)


def put_split(t_ref, col, value):
    hi = value.astype(BF)
    t_ref[0:256, col:col + 128] = hi
    t_ref[256:512, col:col + 128] = (value - hi.astype(F32)).astype(BF)


def table_first(e_ref, step_ref, ta, tb):
    for k in range(3):
        sr, si = step_ref[k, 0], step_ref[k, 1]
        er, ei = e_ref[k, 0, 0], e_ref[k, 0, 1]
        s2r, s2i = sr * sr - si * si, 2.0 * sr * si
        s4r, s4i = s2r * s2r - s2i * s2i, 2.0 * s2r * s2i
        s8r, s8i = s4r * s4r - s4i * s4i, 2.0 * s4r * s4i
        lane = iota((256, 128), 1)
        nyq = jnp.sum(jnp.where(lane == 0, e_ref[k, 1, 0], 0.0), axis=1, keepdims=True)
        put_split(ta, 256 * k, er)
        put_split(ta, 256 * k + 128, jnp.where(lane == 0, nyq, ei))
        put_split(tb, 256 * k, er * s8r - ei * s8i)
        put_split(tb, 256 * k + 128, er * s8i + ei * s8r)


def table_next(half, e_ref, step_ref, t_ref):
    for k in range(3):
        sr, si = step_ref[k, 0], step_ref[k, 1]
        er, ei = e_ref[k, half, 0], e_ref[k, half, 1]
        nr, ni = er * sr - ei * si, er * si + ei * sr
        e_ref[k, half, 0] = nr
        e_ref[k, half, 1] = ni
        put_split(t_ref, 256 * k, nr)
        put_split(t_ref, 256 * k + 128, ni)


def inverse_first(base_ref, w_ref):
    c2 = iota((8, 256), 1)
    r8, i8 = cos_turn(8 * c2, SK)[0:1], sin_turn(8 * c2, SK)[0:1]
    c, s = base_ref[0, 0:128], base_ref[1, 0:128]
    first = iota((128, 256), 0) == 0
    gain = jnp.where(first, 1.0 / 64, 2.0 / 64)
    alt = (1 - 2 * (iota((128, 256), 1) & 1)).astype(F32)
    zero = jnp.zeros((128, 256), BF)
    w_ref[0:128, 0:256] = (c * gain).astype(BF)
    w_ref[0:128, 256:512] = zero
    w_ref[128:256, 0:256] = jnp.where(first, alt * (1.0 / 64), s * (-2.0 / 64)).astype(BF)
    w_ref[128:256, 256:512] = zero
    w_ref[256:384, 0:256] = zero
    w_ref[256:384, 256:512] = ((c * r8 - s * i8) * (2.0 / 64)).astype(BF)
    w_ref[384:512, 0:256] = zero
    w_ref[384:512, 256:512] = ((s * r8 + c * i8) * (-2.0 / 64)).astype(BF)


def inverse_next(g, base_ref, w_ref):
    c2 = iota((8, 256), 1)
    r, i = cos_turn(g * c2, SK)[0:1] * (2.0 / 64), sin_turn(g * c2, SK)[0:1] * (2.0 / 64)
    for half in range(2):
        c, s = base_ref[0, 128 * half:128 * half + 128], base_ref[1, 128 * half:128 * half + 128]
        wr, wi = c * r - s * i, s * r + c * i
        w_ref[256 * half:256 * half + 128, 0:256] = wr.astype(BF)
        w_ref[256 * half:256 * half + 128, 256:512] = wi.astype(BF)
        w_ref[256 * half + 128:256 * half + 256, 0:256] = (-wi).astype(BF)
        w_ref[256 * half + 128:256 * half + 256, 256:512] = wr.astype(BF)


def multiply(rows, first, spec_ref, cube_ref, p_ref, half):
    block = 16
    for n in range(rows // block):
        r = slice(block * n, block * n + block)
        cube = cube_ref[r, :]
        ar, ai, br, bi, cr, ci = [spec_ref[r, 128 * q:128 * q + 128] for q in range(6)]
        ar, ai = ar * cube, ai * cube
        xr, xi = ar * br - ai * bi, ar * bi + ai * br
        yr, yi = xr * cr - xi * ci, xr * ci + xi * cr
        if first:
            lane = iota((block, 128), 1) == 0
            yr = jnp.where(lane, ar * br * cr, yr)
            yi = jnp.where(lane, ai * bi * ci, yi)
        p_ref[r, 256 * half:256 * half + 128] = yr.astype(BF)
        p_ref[r, 256 * half + 128:256 * half + 256] = yi.astype(BF)


def combine(rows, y_ref, f_ref):
    block = 16
    h, C, S = (jnp.float32(v) for v in (math.sqrt(0.5), math.cos(math.pi / 8), math.sin(math.pi / 8)))

    def step(n, carry):
        r = pl.ds(pl.multiple_of(n * block, block), block)
        for half in range(2):
            lo = slice(128 * half, 128 * half + 128)
            hi = slice(256 + 128 * half, 256 + 128 * half + 128)
            re = lambda g: y_ref[g, r, lo]
            im = lambda g: y_ref[g, r, hi]
            y0, y8 = re(0), im(0)
            a, b = y0 + y8, y0 - y8
            r4, i4 = re(4), im(4)
            ee = [a + r4, b - i4, a - r4, b + i4]
            r2, i2, r6, i6 = re(2), im(2), re(6), im(6)
            d, e = h * (r2 - r6), h * (i2 + i6)
            eo = [r2 + r6, d - e, i6 - i2, -d - e]
            even = [ee[q] + eo[q] for q in range(4)] + [ee[q] - eo[q] for q in range(4)]
            r1, r7, i1, i7 = re(1), re(7), im(1), im(7)
            r3, r5, i3, i5 = re(3), re(5), im(3), im(5)
            p1, m1, q1, n1 = r1 + r7, r1 - r7, i1 - i7, i1 + i7
            p3, m3, q3, n3 = r3 + r5, r3 - r5, i3 - i5, i3 + i5
            dp, dq = h * (p1 - p3), h * (q1 + q3)
            u1, v1 = m1 * C + m3 * S, n1 * S + n3 * C
            u3, v3 = m1 * S - m3 * C, n1 * C - n3 * S
            odd = [p1 + p3, u1 - v1, dp - dq, u3 - v3, q3 - q1, -u3 - v3, -dp - dq, -u1 - v1]
            for q in range(8):
                f_ref[q, r, lo] = (even[q] + odd[q]).astype(BF)
                f_ref[q + 8, r, lo] = (even[q] - odd[q]).astype(BF)
        return carry

    lax.fori_loop(0, rows // block, step, 0)


def dot(a, b):
    return jnp.dot(a, b, preferred_element_type=F32)


def features(rows, x2, cube, e_ref, step_ref, base_ref, ta, tb, w_ref, sa, sb, p_ref, y_ref, f_ref):
    table_first(e_ref, step_ref, ta, tb)
    sa[...] = dot(x2[...], ta[...])
    inverse_first(base_ref, w_ref)
    sb[...] = dot(x2[...], tb[...])
    multiply(rows, True, sa, cube, p_ref, 0)
    table_next(0, e_ref, step_ref, ta)

    def step(g, carry):
        sa[...] = dot(x2[...], ta[...])
        multiply(rows, False, sb, cube, p_ref, 1)
        table_next(1, e_ref, step_ref, tb)
        y_ref[g - 1] = dot(p_ref[...], w_ref[...])
        sb[...] = dot(x2[...], tb[...])
        multiply(rows, False, sa, cube, p_ref, 0)
        table_next(0, e_ref, step_ref, ta)
        inverse_next(g, base_ref, w_ref)
        return carry

    lax.fori_loop(1, 8, step, 0)
    multiply(rows, False, sb, cube, p_ref, 1)
    y_ref[7] = dot(p_ref[...], w_ref[...])
    combine(rows, y_ref, f_ref)


def scratch(rows):
    return [
        pltpu.VMEM((rows, 512), BF),
        pltpu.VMEM((rows, 128), F32),
        pltpu.VMEM((3, 2, 2, 256, 128), F32),
        pltpu.VMEM((3, 2, 256, 128), F32),
        pltpu.VMEM((2, 256, 256), F32),
        pltpu.VMEM((512, 768), BF),
        pltpu.VMEM((512, 768), BF),
        pltpu.VMEM((512, 512), BF),
        pltpu.VMEM((rows, 768), F32),
        pltpu.VMEM((rows, 768), F32),
        pltpu.VMEM((rows, 512), BF),
        pltpu.VMEM((8, rows, 512), F32),
        pltpu.VMEM((16, rows, 256), BF),
    ]


def sketch(rows, bid_ref, sign_ref, x2, cube, e_ref, step_ref, base_ref, ta, tb, w_ref, sa, sb, p_ref, y_ref, f_ref):
    setup(bid_ref, sign_ref, e_ref, step_ref, base_ref)
    features(rows, x2, cube, e_ref, step_ref, base_ref, ta, tb, w_ref, sa, sb, p_ref, y_ref, f_ref)


MESH = pl.DeviceIdType.MESH


def fused_kernel(rows, x_hbm, target_hbm, count_hbm, bid_hbm, sign_hbm, gram_ref, zty_ref,
                 x_ref, target_ref, count_ref, bid_ref, sign_ref, in_sem, *refs):
    inputs = [pltpu.make_async_copy(src, dst, in_sem.at[i]) for i, (src, dst) in enumerate((
        (bid_hbm, bid_ref), (sign_hbm, sign_ref), (count_hbm, count_ref), (x_hbm, x_ref), (target_hbm, target_ref)))]
    for copy in inputs:
        copy.start()
    (half, mine, sib, tx, rx, zown, sibz, zpair, zx, zall,
     sib_send, sib_recv, send, recv, z_send, z_recv) = refs[-16:]
    x2, cube, f_ref = refs[0], refs[1], refs[-17]
    d = lax.axis_index("dp")
    core, lane, ring = d % 2, (d // 2) % 2, d // 4

    def device(turn, other):
        return 4 * ((ring + turn) % 4) + 2 * ((lane + other) % 2) + core

    def choose(first, second):
        return first * (1 - core) + second * core

    sibling = d + 1 - 2 * core
    across, one, two, three = device(0, 1), device(1, 0), device(2, 0), device(3, 0)
    neighbours = (sibling, across, one, two, three)
    barrier = pltpu.get_barrier_semaphore()
    for peer in neighbours:
        pl.semaphore_signal(barrier, inc=1, device_id={"dp": peer}, device_id_type=MESH)

    def remote(src, dst, send_sem, recv_sem, peer):
        return pltpu.make_async_remote_copy(
            src_ref=src, dst_ref=dst, send_sem=send_sem, recv_sem=recv_sem,
            device_id={"dp": peer}, device_id_type=MESH)

    for copy in inputs:
        copy.wait()
    live = count_ref[d]
    xf = jnp.where(iota((rows, 256), 0) < live, x_ref[...].astype(F32), 0.0)
    s = lax.rsqrt(jnp.mean(xf * xf, axis=1, keepdims=True) + 1e-6) * (1.0 / 16)
    cube[...] = jnp.broadcast_to(s * s * s, (rows, 128))
    x2[:, 0:256] = xf.astype(BF)
    x2[:, 256:512] = xf.astype(BF)
    sketch(rows, bid_ref, sign_ref, *refs[:-16])

    own = f_ref[lax.axis_index("feat")]
    target = jnp.concatenate(
        [jnp.broadcast_to(target_ref[n:n + 1, :].astype(F32), (8, 128)) for n in range(rows // 128)],
        axis=1).astype(BF)
    zown[...] = dot(target, own)
    turned = own.astype(F32).T.astype(BF)
    pl.semaphore_wait(barrier, len(neighbours))

    lanes_first = ((2, 1), (1, 1), (3, 1), (0, 1), (2, 0), (1, 0), (3, 0), (0, 0))
    rings_first = ((2, 1), (2, 0), (1, 1), (1, 0), (3, 1), (3, 0), (0, 1), (0, 0))
    zero_chip = [(device(*at) - core) for at in lanes_first]
    one_chip = [(device(*at) - core) for at in rings_first]
    peers = [choose(a, b) for a, b in zip(
        (across, across, across, across, two, one, three), (two, two, one, one, three, three, across))]
    pair = [remote(half.at[i], sib.at[i], sib_send.at[i], sib_recv.at[i], sibling) for i in range(8)]
    message = [remote(tx.at[i], rx.at[i], send.at[i], recv.at[i], peers[i]) for i in range(7)]
    z_pair = remote(zown, sibz, z_send.at[0], z_recv.at[0], sibling)
    z_lane = remote(zpair, zx, z_send.at[1], z_recv.at[1], across)
    z_ring = [remote(zall.at[ring], zall.at[ring], z_send.at[2 + i], z_recv.at[2 + i], peer)
              for i, peer in enumerate((one, two, three))]

    def finish(k):
        pair[k].wait_recv()
        total = mine[k] + sib[k].astype(F32)
        if k < 6:
            tx[k] = total.astype(BF)
        if k > 3:
            mine[k] = total

    def begin(k):
        if k < 4:
            message[k].start()
        elif k < 6:
            @pl.when(core == 1)
            def _():
                message[k].start()

    for i in range(8):
        half[i] = dot(turned, f_ref[choose(one_chip[i] + 1, zero_chip[i])]).astype(BF)
        if i == 0:
            z_pair.start()
        if i >= 2:
            begin(i - 2)
        mine[i] = dot(turned, f_ref[choose(zero_chip[i], one_chip[i] + 1)])
        pair[i].start()
        if i >= 1:
            finish(i - 1)
        if i == 3:
            z_pair.wait_recv()
            zpair[...] = zown[...] + sibz[...]
        if i == 4:
            z_lane.start()
    finish(7)

    @pl.when(core == 0)
    def _():
        for k in range(3):
            message[k].wait_recv()
            tx[4 + k] = (mine[4 + k] + rx[k].astype(F32)).astype(BF)
            if k > 0:
                message[3 + k].start()
        message[3].wait_recv()
        mine[0] = mine[7] + rx[3].astype(F32)
        message[6].start()

    @pl.when(core == 1)
    def _():
        for k in (0, 2, 4):
            message[k].wait_recv()
        tx[6] = (mine[6] + rx[0].astype(F32) + rx[2].astype(F32) + rx[4].astype(F32)).astype(BF)
        for k in (1, 3):
            message[k].wait_recv()
        mine[0] = mine[7] + rx[1].astype(F32) + rx[3].astype(F32)
        message[6].start()

    z_lane.wait_recv()
    zall[ring] = zpair[...] + zx[...]

    @pl.when(core == 0)
    def _():
        for copy in z_ring:
            copy.start()
        message[4].wait_recv()
        message[5].wait_recv()
        mine[0] = mine[0] + rx[4].astype(F32) + rx[5].astype(F32)

    @pl.when(core == 1)
    def _():
        for copy in z_ring:
            copy.start()
        message[5].wait_recv()
        mine[0] = mine[0] + rx[5].astype(F32)

    for copy in z_ring:
        copy.wait_recv()
    zty_ref[...] = ((zall[0] + zall[1]) + (zall[2] + zall[3]))[0:1] * jnp.float32(6144 ** -0.5)
    message[6].wait_recv()
    gram_ref[...] = (mine[0] + rx[6].astype(F32)).T * jnp.float32(1.0 / 6144)
    for copy in pair + message + [z_pair, z_lane] + z_ring:
        copy.wait_send()


def fused_call(rows):
    vmem = pl.BlockSpec(memory_space=pltpu.VMEM)
    dma = pltpu.SemaphoreType.DMA
    return pl.pallas_call(
        functools.partial(fused_kernel, rows),
        out_shape=(jax.ShapeDtypeStruct((256, 256), F32), jax.ShapeDtypeStruct((1, 256), F32)),
        in_specs=[pl.BlockSpec(memory_space=pltpu.HBM)] * 5,
        out_specs=[vmem, vmem],
        scratch_shapes=[
            pltpu.VMEM((rows, 256), BF),
            pltpu.VMEM((rows // 128, 128), BF),
            pltpu.SMEM((16,), I32),
            pltpu.VMEM((3, 256), I32),
            pltpu.VMEM((3, 256), I32),
            dma((5,)),
        ] + scratch(rows) + [
            pltpu.VMEM((8, 256, 256), BF),
            pltpu.VMEM((8, 256, 256), F32),
            pltpu.VMEM((8, 256, 256), BF),
            pltpu.VMEM((7, 256, 256), BF),
            pltpu.VMEM((7, 256, 256), BF),
            pltpu.VMEM((8, 256), F32),
            pltpu.VMEM((8, 256), F32),
            pltpu.VMEM((8, 256), F32),
            pltpu.VMEM((8, 256), F32),
            pltpu.VMEM((4, 8, 256), F32),
            dma((8,)), dma((8,)), dma((7,)), dma((7,)), dma((5,)), dma((5,)),
        ],
        compiler_params=pltpu.CompilerParams(
            collective_id=0, has_side_effects=True, vmem_limit_bytes=46 << 20),
        name="fused",
    )


def body(samples, targets, counts, bucket_ids, sign_bits):
    rows = samples.shape[0]
    operands = (samples, targets.reshape(rows // 128, 128), counts, bucket_ids, sign_bits)
    gram, zty = fused_call(rows)(
        *[pltpu.with_memory_space_constraint(value, pltpu.HBM) for value in operands])
    return gram, zty.reshape(256)


def solution(mesh):
    placed = (P("dp", None), P("dp"), P(), P(), P())
    return jax.shard_map(
        body, mesh=mesh, in_specs=placed, out_specs=(P("dp", "feat"), P("feat")), check_vma=False
    )
```

```python
import functools, math
import jax, jax.numpy as jnp
from jax import lax
from jax.experimental import pallas as pl
from jax.experimental.pallas import tpu as pltpu
from jax.sharding import PartitionSpec as P

F32, BF, I32 = jnp.float32, jnp.bfloat16, jnp.int32
SK = 4096


def sin_poly(t):
    u = t * t
    p = jnp.float32(2.6019031e-06)
    p = p * u + jnp.float32(-1.9807414e-04)
    p = p * u + jnp.float32(8.3330255e-03)
    p = p * u + jnp.float32(-1.6666657e-01)
    return t + t * (u * p)


def sin_turn(n, period):
    quarter = period // 4
    m = ((n + quarter) & (period - 1)) - quarter
    m = jnp.where(m > quarter, period // 2 - m, m)
    return sin_poly(m.astype(F32) * jnp.float32(2.0 * math.pi / period))


def cos_turn(n, period):
    return sin_turn(n + period // 4, period)


def iota(shape, dim):
    return lax.broadcasted_iota(I32, shape, dim)


def dot(a, b):
    return jnp.dot(a, b, preferred_element_type=F32)


EVEN, ODD = (2, 4, 6, 8, 10, 12, 14), (1, 3, 5, 7, 9, 11, 13, 15)


def column(k, bid_ref, sign_ref):
    packed = bid_ref[k:k + 1, :] + SK * sign_ref[k:k + 1, :]
    eye = iota((256, 256), 0) == iota((256, 256), 1)
    both = jnp.sum(jnp.where(eye, packed.astype(F32), 0.0), axis=1, keepdims=True)
    both = jnp.broadcast_to(both, (256, 128)).astype(I32)
    return both & (SK - 1), (2 * (both >> 12) - 1).astype(F32)


def put_split(t_ref, col, value):
    hi = value.astype(BF)
    t_ref[0:256, col:col + 128] = hi
    t_ref[256:512, col:col + 128] = (value - hi.astype(F32)).astype(BF)


def table_first(k, bid_ref, sign_ref, e_ref, step_ref, t_ref):
    b, s = column(k, bid_ref, sign_ref)
    lane = iota((256, 128), 1)
    er, ei = s * cos_turn(b * lane, 128), -s * sin_turn(b * lane, 128)
    e_ref[k, 0] = er
    e_ref[k, 1] = ei
    sr, si = cos_turn(b * lane, SK), -sin_turn(b * lane, SK)
    step_ref[k, 0] = sr
    step_ref[k, 1] = si
    flip = (1 - 2 * (b & 1)).astype(F32)
    hr, hi = flip * sr[:, 16:17], flip * si[:, 16:17]
    low = lane < 64
    put_split(t_ref, 256 * k, jnp.where(low, er, er * hr - ei * hi))
    put_split(t_ref, 256 * k + 128, jnp.where(lane == 0, s * flip, jnp.where(low, ei, er * hi + ei * hr)))


def table_next(k, g, e_ref, step_ref, t_ref):
    sr, si = step_ref[k, 0, :, g:g + 1], step_ref[k, 1, :, g:g + 1]
    er, ei = e_ref[k, 0], e_ref[k, 1]
    put_split(t_ref, 256 * k, er * sr - ei * si)
    put_split(t_ref, 256 * k + 128, er * si + ei * sr)


def inverse_first(base_ref, w_ref):
    n = iota((128, 128), 0) * iota((128, 128), 1)
    base_ref[0] = cos_turn(n, 128)
    base_ref[1] = sin_turn(n, 128)
    row = iota((128, 128), 0)
    c2 = iota((128, 128), 1)
    low = row < 64
    f = jnp.where(low, 32 * row, 16 + 32 * (row - 64))
    gain = jnp.where(row == 0, 1.0 / 64, 2.0 / 64)
    wr = cos_turn(f * c2, SK) * gain
    wi = sin_turn(f * c2, SK) * (-2.0 / 64)
    wi = jnp.where(row == 0, (1 - 2 * (c2 & 1)).astype(F32) * (1.0 / 64), wi)
    for at, w in ((0, wr), (128, wi)):
        w_ref[at:at + 128, 0:128] = jnp.where(low, w, 0.0).astype(BF)
        w_ref[at:at + 128, 128:256] = jnp.where(low, 0.0, w).astype(BF)


def inverse_next(g, base_ref, w_ref):
    c2 = iota((8, 128), 1)
    r, i = cos_turn(g * c2, SK)[0:1] * (2.0 / 64), sin_turn(g * c2, SK)[0:1] * (2.0 / 64)
    c, s = base_ref[0], base_ref[1]
    wr, wi = c * r - s * i, s * r + c * i
    w_ref[0:128, 0:128] = wr.astype(BF)
    w_ref[0:128, 128:256] = wi.astype(BF)
    w_ref[128:256, 0:128] = (-wi).astype(BF)
    w_ref[128:256, 128:256] = wr.astype(BF)


def multiply(rows, first, spec_ref, cube_ref, p_ref):
    block = 16
    for n in range(rows // block):
        r = slice(block * n, block * n + block)
        cube = cube_ref[r, :]
        ar, ai, br, bi, cr, ci = [spec_ref[r, 128 * q:128 * q + 128] for q in range(6)]
        ar, ai = ar * cube, ai * cube
        xr, xi = ar * br - ai * bi, ar * bi + ai * br
        yr, yi = xr * cr - xi * ci, xr * ci + xi * cr
        if first:
            lane = iota((block, 128), 1) == 0
            yr = jnp.where(lane, ar * br * cr, yr)
            yi = jnp.where(lane, ai * bi * ci, yi)
        p_ref[r, 0:128] = yr.astype(BF)
        p_ref[r, 128:256] = yi.astype(BF)


def real_sixteen(y0, y8, re, im):
    h, C, S = (jnp.float32(v) for v in (math.sqrt(0.5), math.cos(math.pi / 8), math.sin(math.pi / 8)))
    a, b = y0 + y8, y0 - y8
    r4, i4 = re(4), im(4)
    ee = [a + r4, b - i4, a - r4, b + i4]
    r2, i2, r6, i6 = re(2), im(2), re(6), im(6)
    d, e = h * (r2 - r6), h * (i2 + i6)
    eo = [r2 + r6, d - e, i6 - i2, -d - e]
    even = [ee[q] + eo[q] for q in range(4)] + [ee[q] - eo[q] for q in range(4)]
    r1, r7, i1, i7 = re(1), re(7), im(1), im(7)
    r3, r5, i3, i5 = re(3), re(5), im(3), im(5)
    p1, m1, q1, n1 = r1 + r7, r1 - r7, i1 - i7, i1 + i7
    p3, m3, q3, n3 = r3 + r5, r3 - r5, i3 - i5, i3 + i5
    dp, dq = h * (p1 - p3), h * (q1 + q3)
    u1, v1 = m1 * C + m3 * S, n1 * S + n3 * C
    u3, v3 = m1 * S - m3 * C, n1 * C - n3 * S
    odd = [p1 + p3, u1 - v1, dp - dq, u3 - v3, q3 - q1, -u3 - v3, -dp - dq, -u1 - v1]
    return [even[q] + odd[q] for q in range(8)] + [even[q] - odd[q] for q in range(8)]


def combine_even(start, stop, y_ref):
    for n in range(start, stop):
        r = slice(8 * n, 8 * n + 8)
        out = real_sixteen(y_ref[0, r, 0:128], y_ref[0, r, 128:256],
                           lambda g: y_ref[g, r, 0:128], lambda g: y_ref[g, r, 128:256])
        for q in range(16):
            y_ref[q // 2, r, 128 * (q % 2):128 * (q % 2) + 128] = out[q]


def combine_odd(rows, y_ref, f_ref):
    block = 16
    cos = lambda n: jnp.float32(math.cos(math.pi * n / 16))
    sin = lambda n: jnp.float32(math.sin(math.pi * n / 16))
    h, C, S = (jnp.float32(v) for v in (math.sqrt(0.5), math.cos(math.pi / 8), math.sin(math.pi / 8)))

    def put(r, q, value, f_ref):
        lanes = slice(128 * (q % 2), 128 * (q % 2) + 128)
        even = y_ref[q // 2, r, lanes]
        f_ref[q // 2, r, lanes] = (even + value).astype(BF)
        f_ref[8 + q // 2, r, lanes] = (even - value).astype(BF)

    def parts(r, sign):
        re = lambda g: y_ref[8 + g // 2, r, 0:128]
        im = lambda g: y_ref[8 + g // 2, r, 128:256]
        a = {g: re(g) + re(16 - g) if sign > 0 else re(g) - re(16 - g) for g in (1, 3, 5, 7)}
        b = {g: im(g) - im(16 - g) if sign > 0 else im(g) + im(16 - g) for g in (1, 3, 5, 7)}
        return a, b

    def evens(n, carry):
        r = pl.ds(pl.multiple_of(n * block, block), block)
        p, q = parts(r, 1)
        p1, m1, q1, n1 = p[1] + p[7], p[1] - p[7], q[1] - q[7], q[1] + q[7]
        p3, m3, q3, n3 = p[3] + p[5], p[3] - p[5], q[3] - q[5], q[3] + q[5]
        put(r, 0, p1 + p3, f_ref)
        put(r, 8, q3 - q1, f_ref)
        dp, dq = h * (p1 - p3), h * (q1 + q3)
        put(r, 4, dp - dq, f_ref)
        put(r, 12, -dp - dq, f_ref)
        u1, v1 = m1 * C + m3 * S, n1 * S + n3 * C
        put(r, 2, u1 - v1, f_ref)
        put(r, 14, -u1 - v1, f_ref)
        u3, v3 = m1 * S - m3 * C, n1 * C - n3 * S
        put(r, 6, u3 - v3, f_ref)
        put(r, 10, -u3 - v3, f_ref)
        return carry

    def odds(n, carry):
        r = pl.ds(pl.multiple_of(n * block, block), block)
        m, w = parts(r, -1)
        for c in (1, 3, 5, 7):
            u = m[1] * cos(c) + m[3] * cos(3 * c) + m[5] * cos(5 * c) + m[7] * cos(7 * c)
            v = w[1] * sin(c) + w[3] * sin(3 * c) + w[5] * sin(5 * c) + w[7] * sin(7 * c)
            put(r, c, u - v, f_ref)
            put(r, 16 - c, -u - v, f_ref)
        return carry

    lax.fori_loop(0, rows // block, evens, 0, unroll=2)
    lax.fori_loop(0, rows // block, odds, 0, unroll=2)


def sketch(rows, bid_ref, sign_ref, x2, cube, e_ref, step_ref, base_ref, ta, tb, wa, wb, sa, sb, pa, pb,
           y_ref, f_ref):
    inverse_first(base_ref, wa)
    for k in range(3):
        table_first(k, bid_ref, sign_ref, e_ref, step_ref, ta)
        lanes = slice(256 * k, 256 * k + 256)
        sa[:, lanes] = dot(x2[...], ta[:, lanes])
    groups = EVEN + ODD
    slots = [0] + [g // 2 + 8 * (g % 2) for g in groups]
    for k in range(3):
        table_next(k, groups[0], e_ref, step_ref, tb)
    inverse_next(groups[0], base_ref, wb)
    bufs = ((ta, wa, sa, pa), (tb, wb, sb, pb))
    blocks = rows // 8
    for n in range(1, 16):
        t, w, s, p = bufs[n % 2]
        t_old, w_old, s_old, p_old = bufs[(n + 1) % 2]
        s[...] = dot(x2[...], t[...])
        multiply(rows, n == 1, s_old, cube, p_old)
        if n < 15:
            g = groups[n]
            for k in range(3):
                table_next(k, g, e_ref, step_ref, t_old)
        y_ref[slots[n - 1]] = dot(p_old[...], w_old[...])
        if n < 15:
            inverse_next(g, base_ref, w_old)
        if n >= 9 and n < 15:
            combine_even(blocks * (n - 9) // 6, blocks * (n - 8) // 6, y_ref)
    multiply(rows, False, sb, cube, pb)
    y_ref[slots[15]] = dot(pb[...], wb[...])
    combine_odd(rows, y_ref, f_ref)


def scratch(rows):
    return [
        pltpu.VMEM((rows, 512), BF),
        pltpu.VMEM((rows, 128), F32),
        pltpu.VMEM((3, 2, 256, 128), F32),
        pltpu.VMEM((3, 2, 256, 128), F32),
        pltpu.VMEM((2, 128, 128), F32),
        pltpu.VMEM((512, 768), BF),
        pltpu.VMEM((512, 768), BF),
        pltpu.VMEM((256, 256), BF),
        pltpu.VMEM((256, 256), BF),
        pltpu.VMEM((rows, 768), F32),
        pltpu.VMEM((rows, 768), F32),
        pltpu.VMEM((rows, 256), BF),
        pltpu.VMEM((rows, 256), BF),
        pltpu.VMEM((16, rows, 256), F32),
        pltpu.VMEM((16, rows, 256), BF),
    ]


MESH = pl.DeviceIdType.MESH


def fused_kernel(rows, x_hbm, target_hbm, count_hbm, bid_hbm, sign_hbm, gram_ref, zty_ref,
                 x_ref, target_ref, count_ref, bid_ref, sign_ref, in_sem, *refs):
    inputs = [pltpu.make_async_copy(src, dst, in_sem.at[i]) for i, (src, dst) in enumerate((
        (bid_hbm, bid_ref), (sign_hbm, sign_ref), (count_hbm, count_ref), (x_hbm, x_ref), (target_hbm, target_ref)))]
    for copy in inputs:
        copy.start()
    (half, mine, sib, tx, rx, zown, sibz, zpair, zx, zall,
     sib_send, sib_recv, send, recv, z_send, z_recv) = refs[-16:]
    x2, cube, f_ref = refs[0], refs[1], refs[-17]
    d = lax.axis_index("dp")
    core, lane, ring = d % 2, (d // 2) % 2, d // 4

    def device(turn, other):
        return 4 * ((ring + turn) % 4) + 2 * ((lane + other) % 2) + core

    def choose(first, second):
        return first * (1 - core) + second * core

    sibling = d + 1 - 2 * core
    across, one, two, three = device(0, 1), device(1, 0), device(2, 0), device(3, 0)
    neighbours = (sibling, across, one, two, three)
    barrier = pltpu.get_barrier_semaphore()
    for peer in neighbours:
        pl.semaphore_signal(barrier, inc=1, device_id={"dp": peer}, device_id_type=MESH)

    def remote(src, dst, send_sem, recv_sem, peer):
        return pltpu.make_async_remote_copy(
            src_ref=src, dst_ref=dst, send_sem=send_sem, recv_sem=recv_sem,
            device_id={"dp": peer}, device_id_type=MESH)

    for copy in inputs:
        copy.wait()
    live = count_ref[d]
    xf = jnp.where(iota((rows, 256), 0) < live, x_ref[...].astype(F32), 0.0)
    s = lax.rsqrt(jnp.mean(xf * xf, axis=1, keepdims=True) + 1e-6) * (1.0 / 16)
    cube[...] = jnp.broadcast_to(s * s * s, (rows, 128))
    x2[:, 0:256] = xf.astype(BF)
    x2[:, 256:512] = xf.astype(BF)
    sketch(rows, bid_ref, sign_ref, *refs[:-16])

    own = f_ref[lax.axis_index("feat")]
    target = jnp.concatenate(
        [jnp.broadcast_to(target_ref[n:n + 1, :].astype(F32), (8, 128)) for n in range(rows // 128)],
        axis=1).astype(BF)
    zown[...] = dot(target, own)
    turned = own.astype(F32).T.astype(BF)
    pl.semaphore_wait(barrier, len(neighbours))

    lanes_first = ((2, 1), (1, 1), (3, 1), (0, 1), (2, 0), (1, 0), (3, 0), (0, 0))
    rings_first = ((2, 1), (2, 0), (1, 1), (1, 0), (3, 1), (3, 0), (0, 1), (0, 0))
    zero_chip = [(device(*at) - core) for at in lanes_first]
    one_chip = [(device(*at) - core) for at in rings_first]
    peers = [choose(a, b) for a, b in zip(
        (across, across, across, across, two, one, three), (two, two, one, one, three, three, across))]
    pair = [remote(half.at[i], sib.at[i], sib_send.at[i], sib_recv.at[i], sibling) for i in range(8)]
    message = [remote(tx.at[i], rx.at[i], send.at[i], recv.at[i], peers[i]) for i in range(7)]
    z_pair = remote(zown, sibz, z_send.at[0], z_recv.at[0], sibling)
    z_lane = remote(zpair, zx, z_send.at[1], z_recv.at[1], across)
    z_ring = [remote(zall.at[ring], zall.at[ring], z_send.at[2 + i], z_recv.at[2 + i], peer)
              for i, peer in enumerate((one, two, three))]

    def finish(k):
        pair[k].wait_recv()
        total = mine[k] + sib[k].astype(F32)
        if k < 6:
            tx[k] = total.astype(BF)
        if k > 3:
            mine[k] = total

    def begin(k):
        if k < 4:
            message[k].start()
        elif k < 6:
            @pl.when(core == 1)
            def _():
                message[k].start()

    for i in range(8):
        half[i] = dot(turned, f_ref[choose(one_chip[i] + 1, zero_chip[i])]).astype(BF)
        if i == 0:
            z_pair.start()
        if i >= 2:
            begin(i - 2)
        mine[i] = dot(turned, f_ref[choose(zero_chip[i], one_chip[i] + 1)])
        pair[i].start()
        if i >= 1:
            finish(i - 1)
        if i == 3:
            z_pair.wait_recv()
            zpair[...] = zown[...] + sibz[...]
        if i == 4:
            z_lane.start()
    finish(7)

    @pl.when(core == 0)
    def _():
        for k in range(3):
            message[k].wait_recv()
            tx[4 + k] = (mine[4 + k] + rx[k].astype(F32)).astype(BF)
            if k > 0:
                message[3 + k].start()
        message[3].wait_recv()
        mine[0] = mine[7] + rx[3].astype(F32)
        message[6].start()

    @pl.when(core == 1)
    def _():
        for k in (0, 2, 4):
            message[k].wait_recv()
        tx[6] = (mine[6] + rx[0].astype(F32) + rx[2].astype(F32) + rx[4].astype(F32)).astype(BF)
        for k in (1, 3):
            message[k].wait_recv()
        mine[0] = mine[7] + rx[1].astype(F32) + rx[3].astype(F32)
        message[6].start()

    z_lane.wait_recv()
    zall[ring] = zpair[...] + zx[...]

    @pl.when(core == 0)
    def _():
        for copy in z_ring:
            copy.start()
        message[4].wait_recv()
        message[5].wait_recv()
        mine[0] = mine[0] + rx[4].astype(F32) + rx[5].astype(F32)

    @pl.when(core == 1)
    def _():
        for copy in z_ring:
            copy.start()
        message[5].wait_recv()
        mine[0] = mine[0] + rx[5].astype(F32)

    for copy in z_ring:
        copy.wait_recv()
    zty_ref[...] = ((zall[0] + zall[1]) + (zall[2] + zall[3]))[0:1] * jnp.float32(6144 ** -0.5)
    message[6].wait_recv()
    gram_ref[...] = (mine[0] + rx[6].astype(F32)).T * jnp.float32(1.0 / 6144)
    for copy in pair + message + [z_pair, z_lane] + z_ring:
        copy.wait_send()


def fused_call(rows):
    vmem = pl.BlockSpec(memory_space=pltpu.VMEM)
    dma = pltpu.SemaphoreType.DMA
    return pl.pallas_call(
        functools.partial(fused_kernel, rows),
        out_shape=(jax.ShapeDtypeStruct((256, 256), F32), jax.ShapeDtypeStruct((1, 256), F32)),
        in_specs=[pl.BlockSpec(memory_space=pltpu.HBM)] * 5,
        out_specs=[vmem, vmem],
        scratch_shapes=[
            pltpu.VMEM((rows, 256), BF),
            pltpu.VMEM((rows // 128, 128), BF),
            pltpu.SMEM((16,), I32),
            pltpu.VMEM((3, 256), I32),
            pltpu.VMEM((3, 256), I32),
            dma((5,)),
        ] + scratch(rows) + [
            pltpu.VMEM((8, 256, 256), BF),
            pltpu.VMEM((8, 256, 256), F32),
            pltpu.VMEM((8, 256, 256), BF),
            pltpu.VMEM((7, 256, 256), BF),
            pltpu.VMEM((7, 256, 256), BF),
            pltpu.VMEM((8, 256), F32),
            pltpu.VMEM((8, 256), F32),
            pltpu.VMEM((8, 256), F32),
            pltpu.VMEM((8, 256), F32),
            pltpu.VMEM((4, 8, 256), F32),
            dma((8,)), dma((8,)), dma((7,)), dma((7,)), dma((5,)), dma((5,)),
        ],
        compiler_params=pltpu.CompilerParams(
            collective_id=0, has_side_effects=True, vmem_limit_bytes=46 << 20),
        name="fused",
    )


def body(samples, targets, counts, bucket_ids, sign_bits):
    rows = samples.shape[0]
    operands = (samples, targets.reshape(rows // 128, 128), counts, bucket_ids, sign_bits)
    gram, zty = fused_call(rows)(
        *[pltpu.with_memory_space_constraint(value, pltpu.HBM) for value in operands])
    return gram, zty.reshape(256)


def solution(mesh):
    placed = (P("dp", None), P("dp"), P(), P(), P())
    return jax.shard_map(
        body, mesh=mesh, in_specs=placed, out_specs=(P("dp", "feat"), P("feat")), check_vma=False
    )
```

```python
import functools, math
import jax, jax.numpy as jnp
from jax import lax
from jax.experimental import pallas as pl
from jax.experimental.pallas import tpu as pltpu
from jax.sharding import PartitionSpec as P

F32, BF, I32 = jnp.float32, jnp.bfloat16, jnp.int32
SK = 4096
SPLIT = 2


def sin_poly(t):
    u = t * t
    p = jnp.float32(2.6019031e-06)
    p = p * u + jnp.float32(-1.9807414e-04)
    p = p * u + jnp.float32(8.3330255e-03)
    p = p * u + jnp.float32(-1.6666657e-01)
    return t + t * (u * p)


def sin_turn(n, period):
    quarter = period // 4
    m = ((n + quarter) & (period - 1)) - quarter
    m = jnp.where(m > quarter, period // 2 - m, m)
    return sin_poly(m.astype(F32) * jnp.float32(2.0 * math.pi / period))


def cos_turn(n, period):
    return sin_turn(n + period // 4, period)


def iota(shape, dim):
    return lax.broadcasted_iota(I32, shape, dim)


def dot(a, b):
    return jnp.dot(a, b, preferred_element_type=F32)


EVEN, ODD = (2, 4, 6, 8, 10, 12, 14), (1, 3, 5, 7, 9, 11, 13, 15)


def column(k, bid_ref, sign_ref):
    packed = bid_ref[k:k + 1, :] + SK * sign_ref[k:k + 1, :]
    eye = iota((256, 256), 0) == iota((256, 256), 1)
    both = jnp.sum(jnp.where(eye, packed.astype(F32), 0.0), axis=1, keepdims=True)
    both = jnp.broadcast_to(both, (256, 128)).astype(I32)
    return both & (SK - 1), (2 * (both >> 12) - 1).astype(F32)


def put_split(t_ref, k, part, value):
    col = 256 * k + 128 * part
    hi = value.astype(BF)
    t_ref[0:256, col:col + 128] = hi
    if k < SPLIT:
        t_ref[256:512, col:col + 128] = (value - hi.astype(F32)).astype(BF)


def spectrum(x2, t_ref, k):
    lanes = slice(256 * k, 256 * k + 256)
    depth = 512 if k < SPLIT else 256
    return dot(x2[:, 0:depth], t_ref[0:depth, lanes])


def table_first(k, bid_ref, sign_ref, e_ref, step_ref, t_ref):
    b, s = column(k, bid_ref, sign_ref)
    lane = iota((256, 128), 1)
    er, ei = s * cos_turn(b * lane, 128), -s * sin_turn(b * lane, 128)
    e_ref[k, 0] = er
    e_ref[k, 1] = ei
    sr, si = cos_turn(b * lane, SK), -sin_turn(b * lane, SK)
    step_ref[k, 0] = sr
    step_ref[k, 1] = si
    flip = (1 - 2 * (b & 1)).astype(F32)
    hr, hi = flip * sr[:, 16:17], flip * si[:, 16:17]
    low = lane < 64
    put_split(t_ref, k, 0, jnp.where(low, er, er * hr - ei * hi))
    put_split(t_ref, k, 1, jnp.where(lane == 0, s * flip, jnp.where(low, ei, er * hi + ei * hr)))


def table_next(k, g, e_ref, step_ref, t_ref):
    sr, si = step_ref[k, 0, :, g:g + 1], step_ref[k, 1, :, g:g + 1]
    er, ei = e_ref[k, 0], e_ref[k, 1]
    put_split(t_ref, k, 0, er * sr - ei * si)
    put_split(t_ref, k, 1, er * si + ei * sr)


def inverse_first(base_ref, w_ref):
    n = iota((128, 128), 0) * iota((128, 128), 1)
    base_ref[0] = cos_turn(n, 128)
    base_ref[1] = sin_turn(n, 128)
    row = iota((128, 128), 0)
    c2 = iota((128, 128), 1)
    low = row < 64
    f = jnp.where(low, 32 * row, 16 + 32 * (row - 64))
    gain = jnp.where(row == 0, 1.0 / 64, 2.0 / 64)
    wr = cos_turn(f * c2, SK) * gain
    wi = sin_turn(f * c2, SK) * (-2.0 / 64)
    wi = jnp.where(row == 0, (1 - 2 * (c2 & 1)).astype(F32) * (1.0 / 64), wi)
    for at, w in ((0, wr), (128, wi)):
        w_ref[at:at + 128, 0:128] = jnp.where(low, w, 0.0).astype(BF)
        w_ref[at:at + 128, 128:256] = jnp.where(low, 0.0, w).astype(BF)


def inverse_next(g, base_ref, w_ref):
    c2 = iota((8, 128), 1)
    r, i = cos_turn(g * c2, SK)[0:1] * (2.0 / 64), sin_turn(g * c2, SK)[0:1] * (2.0 / 64)
    c, s = base_ref[0], base_ref[1]
    wr, wi = c * r - s * i, s * r + c * i
    w_ref[0:128, 0:128] = wr.astype(BF)
    w_ref[0:128, 128:256] = wi.astype(BF)
    w_ref[128:256, 0:128] = (-wi).astype(BF)
    w_ref[128:256, 128:256] = wr.astype(BF)


def multiply(rows, first, spec_ref, cube_ref, p_ref):
    block = 16
    for n in range(rows // block):
        r = slice(block * n, block * n + block)
        cube = cube_ref[r, :]
        ar, ai, br, bi, cr, ci = [spec_ref[r, 128 * q:128 * q + 128] for q in range(6)]
        ar, ai = ar * cube, ai * cube
        xr, xi = ar * br - ai * bi, ar * bi + ai * br
        yr, yi = xr * cr - xi * ci, xr * ci + xi * cr
        if first:
            lane = iota((block, 128), 1) == 0
            yr = jnp.where(lane, ar * br * cr, yr)
            yi = jnp.where(lane, ai * bi * ci, yi)
        p_ref[r, 0:128] = yr.astype(BF)
        p_ref[r, 128:256] = yi.astype(BF)


def real_sixteen(y0, y8, re, im):
    h, C, S = (jnp.float32(v) for v in (math.sqrt(0.5), math.cos(math.pi / 8), math.sin(math.pi / 8)))
    a, b = y0 + y8, y0 - y8
    r4, i4 = re(4), im(4)
    ee = [a + r4, b - i4, a - r4, b + i4]
    r2, i2, r6, i6 = re(2), im(2), re(6), im(6)
    d, e = h * (r2 - r6), h * (i2 + i6)
    eo = [r2 + r6, d - e, i6 - i2, -d - e]
    even = [ee[q] + eo[q] for q in range(4)] + [ee[q] - eo[q] for q in range(4)]
    r1, r7, i1, i7 = re(1), re(7), im(1), im(7)
    r3, r5, i3, i5 = re(3), re(5), im(3), im(5)
    p1, m1, q1, n1 = r1 + r7, r1 - r7, i1 - i7, i1 + i7
    p3, m3, q3, n3 = r3 + r5, r3 - r5, i3 - i5, i3 + i5
    dp, dq = h * (p1 - p3), h * (q1 + q3)
    u1, v1 = m1 * C + m3 * S, n1 * S + n3 * C
    u3, v3 = m1 * S - m3 * C, n1 * C - n3 * S
    odd = [p1 + p3, u1 - v1, dp - dq, u3 - v3, q3 - q1, -u3 - v3, -dp - dq, -u1 - v1]
    return [even[q] + odd[q] for q in range(8)] + [even[q] - odd[q] for q in range(8)]


def combine_even(start, stop, y_ref):
    for n in range(start, stop):
        r = slice(8 * n, 8 * n + 8)
        out = real_sixteen(y_ref[0, r, 0:128], y_ref[0, r, 128:256],
                           lambda g: y_ref[g, r, 0:128], lambda g: y_ref[g, r, 128:256])
        for q in range(16):
            y_ref[q // 2, r, 128 * (q % 2):128 * (q % 2) + 128] = out[q]


def combine_odd(rows, y_ref, f_ref):
    block = 16
    cos = lambda n: jnp.float32(math.cos(math.pi * n / 16))
    sin = lambda n: jnp.float32(math.sin(math.pi * n / 16))
    h, C, S = (jnp.float32(v) for v in (math.sqrt(0.5), math.cos(math.pi / 8), math.sin(math.pi / 8)))

    def put(r, q, value, f_ref):
        lanes = slice(128 * (q % 2), 128 * (q % 2) + 128)
        even = y_ref[q // 2, r, lanes]
        f_ref[q // 2, r, lanes] = (even + value).astype(BF)
        f_ref[8 + q // 2, r, lanes] = (even - value).astype(BF)

    def parts(r, sign):
        re = lambda g: y_ref[8 + g // 2, r, 0:128]
        im = lambda g: y_ref[8 + g // 2, r, 128:256]
        a = {g: re(g) + re(16 - g) if sign > 0 else re(g) - re(16 - g) for g in (1, 3, 5, 7)}
        b = {g: im(g) - im(16 - g) if sign > 0 else im(g) + im(16 - g) for g in (1, 3, 5, 7)}
        return a, b

    def evens(n, carry):
        r = pl.ds(pl.multiple_of(n * block, block), block)
        p, q = parts(r, 1)
        p1, m1, q1, n1 = p[1] + p[7], p[1] - p[7], q[1] - q[7], q[1] + q[7]
        p3, m3, q3, n3 = p[3] + p[5], p[3] - p[5], q[3] - q[5], q[3] + q[5]
        put(r, 0, p1 + p3, f_ref)
        put(r, 8, q3 - q1, f_ref)
        dp, dq = h * (p1 - p3), h * (q1 + q3)
        put(r, 4, dp - dq, f_ref)
        put(r, 12, -dp - dq, f_ref)
        u1, v1 = m1 * C + m3 * S, n1 * S + n3 * C
        put(r, 2, u1 - v1, f_ref)
        put(r, 14, -u1 - v1, f_ref)
        u3, v3 = m1 * S - m3 * C, n1 * C - n3 * S
        put(r, 6, u3 - v3, f_ref)
        put(r, 10, -u3 - v3, f_ref)
        return carry

    def odds(n, carry):
        r = pl.ds(pl.multiple_of(n * block, block), block)
        m, w = parts(r, -1)
        for c in (1, 3, 5, 7):
            u = m[1] * cos(c) + m[3] * cos(3 * c) + m[5] * cos(5 * c) + m[7] * cos(7 * c)
            v = w[1] * sin(c) + w[3] * sin(3 * c) + w[5] * sin(5 * c) + w[7] * sin(7 * c)
            put(r, c, u - v, f_ref)
            put(r, 16 - c, -u - v, f_ref)
        return carry

    lax.fori_loop(0, rows // block, evens, 0, unroll=2)
    lax.fori_loop(0, rows // block, odds, 0, unroll=2)


def sketch(rows, load_rows, bid_ref, sign_ref, x2, cube, e_ref, step_ref, base_ref, ta, tb, wa, wb, sa, sb, pa, pb,
           y_ref, f_ref):
    inverse_first(base_ref, wa)
    for k in range(3):
        table_first(k, bid_ref, sign_ref, e_ref, step_ref, ta)
        if k == 0:
            load_rows()
        sa[:, 256 * k:256 * k + 256] = spectrum(x2, ta, k)
    groups = EVEN + ODD
    slots = [0] + [g // 2 + 8 * (g % 2) for g in groups]
    for k in range(3):
        table_next(k, groups[0], e_ref, step_ref, tb)
    inverse_next(groups[0], base_ref, wb)
    bufs = ((ta, wa, sa, pa), (tb, wb, sb, pb))
    blocks = rows // 8
    for n in range(1, 16):
        t, w, s, p = bufs[n % 2]
        t_old, w_old, s_old, p_old = bufs[(n + 1) % 2]
        for k in range(3):
            s[:, 256 * k:256 * k + 256] = spectrum(x2, t, k)
        multiply(rows, n == 1, s_old, cube, p_old)
        if n < 15:
            g = groups[n]
            for k in range(3):
                table_next(k, g, e_ref, step_ref, t_old)
        y_ref[slots[n - 1]] = dot(p_old[...], w_old[...])
        if n < 15:
            inverse_next(g, base_ref, w_old)
        if n >= 9 and n < 15:
            combine_even(blocks * (n - 9) // 6, blocks * (n - 8) // 6, y_ref)
    multiply(rows, False, sb, cube, pb)
    y_ref[slots[15]] = dot(pb[...], wb[...])
    combine_odd(rows, y_ref, f_ref)


def scratch(rows):
    return [
        pltpu.VMEM((rows, 512), BF),
        pltpu.VMEM((rows, 128), F32),
        pltpu.VMEM((3, 2, 256, 128), F32),
        pltpu.VMEM((3, 2, 256, 128), F32),
        pltpu.VMEM((2, 128, 128), F32),
        pltpu.VMEM((512, 768), BF),
        pltpu.VMEM((512, 768), BF),
        pltpu.VMEM((256, 256), BF),
        pltpu.VMEM((256, 256), BF),
        pltpu.VMEM((rows, 768), F32),
        pltpu.VMEM((rows, 768), F32),
        pltpu.VMEM((rows, 256), BF),
        pltpu.VMEM((rows, 256), BF),
        pltpu.VMEM((16, rows, 256), F32),
        pltpu.VMEM((16, rows, 256), BF),
    ]


MESH = pl.DeviceIdType.MESH


def fused_kernel(rows, x_hbm, target_hbm, count_hbm, bid_hbm, sign_hbm, gram_ref, zty_ref,
                 x_ref, target_ref, count_ref, bid_ref, sign_ref, in_sem, *refs):
    inputs = [pltpu.make_async_copy(src, dst, in_sem.at[i]) for i, (src, dst) in enumerate((
        (bid_hbm, bid_ref), (sign_hbm, sign_ref), (count_hbm, count_ref), (x_hbm, x_ref), (target_hbm, target_ref)))]
    for copy in inputs:
        copy.start()
    (half, mine, sib, tx, rx, zown, sibz, zpair, zx, zall,
     sib_send, sib_recv, send, recv, z_send, z_recv) = refs[-16:]
    x2, cube, f_ref = refs[0], refs[1], refs[-17]
    d = lax.axis_index("dp")
    core, lane, ring = d % 2, (d // 2) % 2, d // 4

    def device(turn, other):
        return 4 * ((ring + turn) % 4) + 2 * ((lane + other) % 2) + core

    def choose(first, second):
        return first * (1 - core) + second * core

    sibling = d + 1 - 2 * core
    across, one, two, three = device(0, 1), device(1, 0), device(2, 0), device(3, 0)
    neighbours = (sibling, across, one, two, three)
    barrier = pltpu.get_barrier_semaphore()
    for peer in neighbours:
        pl.semaphore_signal(barrier, inc=1, device_id={"dp": peer}, device_id_type=MESH)

    def remote(src, dst, send_sem, recv_sem, peer):
        return pltpu.make_async_remote_copy(
            src_ref=src, dst_ref=dst, send_sem=send_sem, recv_sem=recv_sem,
            device_id={"dp": peer}, device_id_type=MESH)

    def load_rows():
        for copy in inputs[2:]:
            copy.wait()
        live = count_ref[d]
        xf = jnp.where(iota((rows, 256), 0) < live, x_ref[...].astype(F32), 0.0)
        s = lax.rsqrt(jnp.mean(xf * xf, axis=1, keepdims=True) + 1e-6) * (1.0 / 16)
        cube[...] = jnp.broadcast_to(s * s * s, (rows, 128))
        x2[:, 0:256] = xf.astype(BF)
        x2[:, 256:512] = xf.astype(BF)

    for copy in inputs[:2]:
        copy.wait()
    sketch(rows, load_rows, bid_ref, sign_ref, *refs[:-16])

    own = f_ref[lax.axis_index("feat")]
    target = jnp.concatenate(
        [jnp.broadcast_to(target_ref[n:n + 1, :].astype(F32), (8, 128)) for n in range(rows // 128)],
        axis=1).astype(BF)
    zown[...] = dot(target, own)
    turned = own.astype(F32).T.astype(BF)
    pl.semaphore_wait(barrier, len(neighbours))

    lanes_first = ((2, 1), (1, 1), (3, 1), (0, 1), (2, 0), (1, 0), (3, 0), (0, 0))
    rings_first = ((2, 1), (1, 1), (3, 1), (2, 0), (1, 0), (3, 0), (0, 1), (0, 0))
    zero_chip = [(device(*at) - core) for at in lanes_first]
    one_chip = [(device(*at) - core) for at in rings_first]
    peers = [choose(a, b) for a, b in zip(
        (across, across, across, across, two, one, three), (two, one, three, two, one, three, across))]
    pair = [remote(half.at[i], sib.at[i], sib_send.at[i], sib_recv.at[i], sibling) for i in range(8)]
    message = [remote(tx.at[i], rx.at[i], send.at[i], recv.at[i], peers[i]) for i in range(7)]
    z_pair = remote(zown, sibz, z_send.at[0], z_recv.at[0], sibling)
    z_lane = remote(zpair, zx, z_send.at[1], z_recv.at[1], across)
    z_ring = [remote(zall.at[ring], zall.at[ring], z_send.at[2 + i], z_recv.at[2 + i], peer)
              for i, peer in enumerate((one, two, three))]

    def finish(k):
        pair[k].wait_recv()
        total = mine[k] + sib[k].astype(F32)
        if k < 6:
            tx[k] = total.astype(BF)
        if k > 3:
            mine[k] = total

    def begin(k):
        if k < 4:
            message[k].start()
        elif k < 6:
            @pl.when(core == 1)
            def _():
                message[k].start()

    for i in range(8):
        half[i] = dot(turned, f_ref[choose(one_chip[i] + 1, zero_chip[i])]).astype(BF)
        if i == 0:
            z_pair.start()
        if i >= 2:
            begin(i - 2)
        mine[i] = dot(turned, f_ref[choose(zero_chip[i], one_chip[i] + 1)])
        pair[i].start()
        if i >= 1:
            finish(i - 1)
        if i == 3:
            z_pair.wait_recv()
            zpair[...] = zown[...] + sibz[...]
        if i == 4:
            z_lane.start()
    finish(7)

    @pl.when(core == 0)
    def _():
        for k in range(3):
            message[k].wait_recv()
            tx[4 + k] = (mine[4 + k] + rx[k].astype(F32)).astype(BF)
            if k > 0:
                message[3 + k].start()
        message[3].wait_recv()
        mine[0] = mine[7] + rx[3].astype(F32)
        message[6].start()

    @pl.when(core == 1)
    def _():
        for k in (0, 1, 2):
            message[k].wait_recv()
        tx[6] = (mine[6] + rx[0].astype(F32) + rx[1].astype(F32) + rx[2].astype(F32)).astype(BF)
        message[3].wait_recv()
        mine[0] = mine[7] + rx[3].astype(F32)
        message[6].start()

    z_lane.wait_recv()
    zall[ring] = zpair[...] + zx[...]

    @pl.when(core == 0)
    def _():
        for copy in z_ring:
            copy.start()
        message[4].wait_recv()
        message[5].wait_recv()
        mine[0] = mine[0] + rx[4].astype(F32) + rx[5].astype(F32)

    @pl.when(core == 1)
    def _():
        for copy in z_ring:
            copy.start()
        message[4].wait_recv()
        message[5].wait_recv()
        mine[0] = mine[0] + rx[4].astype(F32) + rx[5].astype(F32)

    for copy in z_ring:
        copy.wait_recv()
    zty_ref[...] = ((zall[0] + zall[1]) + (zall[2] + zall[3]))[0:1] * jnp.float32(6144 ** -0.5)
    message[6].wait_recv()
    gram_ref[...] = (mine[0] + rx[6].astype(F32)).T * jnp.float32(1.0 / 6144)
    for copy in pair + message + [z_pair, z_lane] + z_ring:
        copy.wait_send()


def fused_call(rows):
    vmem = pl.BlockSpec(memory_space=pltpu.VMEM)
    dma = pltpu.SemaphoreType.DMA
    return pl.pallas_call(
        functools.partial(fused_kernel, rows),
        out_shape=(jax.ShapeDtypeStruct((256, 256), F32), jax.ShapeDtypeStruct((1, 256), F32)),
        in_specs=[pl.BlockSpec(memory_space=pltpu.HBM)] * 5,
        out_specs=[vmem, vmem],
        scratch_shapes=[
            pltpu.VMEM((rows, 256), BF),
            pltpu.VMEM((rows // 128, 128), BF),
            pltpu.SMEM((16,), I32),
            pltpu.VMEM((3, 256), I32),
            pltpu.VMEM((3, 256), I32),
            dma((5,)),
        ] + scratch(rows) + [
            pltpu.VMEM((8, 256, 256), BF),
            pltpu.VMEM((8, 256, 256), F32),
            pltpu.VMEM((8, 256, 256), BF),
            pltpu.VMEM((7, 256, 256), BF),
            pltpu.VMEM((7, 256, 256), BF),
            pltpu.VMEM((8, 256), F32),
            pltpu.VMEM((8, 256), F32),
            pltpu.VMEM((8, 256), F32),
            pltpu.VMEM((8, 256), F32),
            pltpu.VMEM((4, 8, 256), F32),
            dma((8,)), dma((8,)), dma((7,)), dma((7,)), dma((5,)), dma((5,)),
        ],
        compiler_params=pltpu.CompilerParams(
            collective_id=0, has_side_effects=True, vmem_limit_bytes=46 << 20),
        name="fused",
    )


def body(samples, targets, counts, bucket_ids, sign_bits):
    rows = samples.shape[0]
    operands = (samples, targets.reshape(rows // 128, 128), counts, bucket_ids, sign_bits)
    gram, zty = fused_call(rows)(
        *[pltpu.with_memory_space_constraint(value, pltpu.HBM) for value in operands])
    return gram, zty.reshape(256)


def solution(mesh):
    placed = (P("dp", None), P("dp"), P(), P(), P())
    return jax.shard_map(
        body, mesh=mesh, in_specs=placed, out_specs=(P("dp", "feat"), P("feat")), check_vma=False
    )
```

```python
import functools, math
import jax, jax.numpy as jnp
from jax import lax
from jax.experimental import pallas as pl
from jax.experimental.pallas import tpu as pltpu
from jax.sharding import PartitionSpec as P

F32, BF, I32 = jnp.float32, jnp.bfloat16, jnp.int32
SK = 4096
SPLIT = 2


def sin_poly(t):
    u = t * t
    p = jnp.float32(2.6019031e-06)
    p = p * u + jnp.float32(-1.9807414e-04)
    p = p * u + jnp.float32(8.3330255e-03)
    p = p * u + jnp.float32(-1.6666657e-01)
    return t + t * (u * p)


def sin_turn(n, period):
    quarter = period // 4
    m = ((n + quarter) & (period - 1)) - quarter
    m = jnp.where(m > quarter, period // 2 - m, m)
    return sin_poly(m.astype(F32) * jnp.float32(2.0 * math.pi / period))


def cos_turn(n, period):
    return sin_turn(n + period // 4, period)


def iota(shape, dim):
    return lax.broadcasted_iota(I32, shape, dim)


def dot(a, b):
    return jnp.dot(a, b, preferred_element_type=F32)


EVEN, ODD = (2, 4, 6, 8, 10, 12, 14), (1, 3, 5, 7, 9, 11, 13, 15)


def column(k, bid_ref, sign_ref):
    packed = bid_ref[k:k + 1, :] + SK * sign_ref[k:k + 1, :]
    eye = iota((256, 256), 0) == iota((256, 256), 1)
    both = jnp.sum(jnp.where(eye, packed.astype(F32), 0.0), axis=1, keepdims=True)
    both = jnp.broadcast_to(both, (256, 128)).astype(I32)
    return both & (SK - 1), (2 * (both >> 12) - 1).astype(F32)


def put_split(t_ref, k, part, value):
    col = 256 * k + 128 * part
    hi = value.astype(BF)
    t_ref[0:256, col:col + 128] = hi
    if k < SPLIT:
        t_ref[256:512, col:col + 128] = (value - hi.astype(F32)).astype(BF)


def spectrum(x2, t_ref, k):
    lanes = slice(256 * k, 256 * k + 256)
    depth = 512 if k < SPLIT else 256
    return dot(x2[:, 0:depth], t_ref[0:depth, lanes])


def table_first(k, bid_ref, sign_ref, e_ref, step_ref, t_ref):
    b, s = column(k, bid_ref, sign_ref)
    lane = iota((256, 128), 1)
    er, ei = s * cos_turn(b * lane, 128), -s * sin_turn(b * lane, 128)
    e_ref[k, 0] = er
    e_ref[k, 1] = ei
    sr, si = cos_turn(b * lane, SK), -sin_turn(b * lane, SK)
    step_ref[k, 0] = sr
    step_ref[k, 1] = si
    flip = (1 - 2 * (b & 1)).astype(F32)
    hr, hi = flip * sr[:, 16:17], flip * si[:, 16:17]
    low = lane < 64
    put_split(t_ref, k, 0, jnp.where(low, er, er * hr - ei * hi))
    put_split(t_ref, k, 1, jnp.where(lane == 0, s * flip, jnp.where(low, ei, er * hi + ei * hr)))


def table_next(k, g, e_ref, step_ref, t_ref):
    sr, si = step_ref[k, 0, :, g:g + 1], step_ref[k, 1, :, g:g + 1]
    er, ei = e_ref[k, 0], e_ref[k, 1]
    put_split(t_ref, k, 0, er * sr - ei * si)
    put_split(t_ref, k, 1, er * si + ei * sr)


def inverse_first(base_ref, w_ref):
    n = iota((128, 128), 0) * iota((128, 128), 1)
    base_ref[0] = cos_turn(n, 128)
    base_ref[1] = sin_turn(n, 128)
    row = iota((128, 128), 0)
    c2 = iota((128, 128), 1)
    low = row < 64
    f = jnp.where(low, 32 * row, 16 + 32 * (row - 64))
    gain = jnp.where(row == 0, 1.0 / 64, 2.0 / 64)
    wr = cos_turn(f * c2, SK) * gain
    wi = sin_turn(f * c2, SK) * (-2.0 / 64)
    wi = jnp.where(row == 0, (1 - 2 * (c2 & 1)).astype(F32) * (1.0 / 64), wi)
    for at, w in ((0, wr), (128, wi)):
        w_ref[at:at + 128, 0:128] = jnp.where(low, w, 0.0).astype(BF)
        w_ref[at:at + 128, 128:256] = jnp.where(low, 0.0, w).astype(BF)


def inverse_next(g, base_ref, w_ref):
    c2 = iota((8, 128), 1)
    r, i = cos_turn(g * c2, SK)[0:1] * (2.0 / 64), sin_turn(g * c2, SK)[0:1] * (2.0 / 64)
    c, s = base_ref[0], base_ref[1]
    wr, wi = c * r - s * i, s * r + c * i
    w_ref[0:128, 0:128] = wr.astype(BF)
    w_ref[0:128, 128:256] = wi.astype(BF)
    w_ref[128:256, 0:128] = (-wi).astype(BF)
    w_ref[128:256, 128:256] = wr.astype(BF)


def multiply(rows, first, spec_ref, cube_ref, p_ref):
    block = 16
    for n in range(rows // block):
        r = slice(block * n, block * n + block)
        cube = cube_ref[r, :]
        ar, ai, br, bi, cr, ci = [spec_ref[r, 128 * q:128 * q + 128] for q in range(6)]
        ar, ai = ar * cube, ai * cube
        xr, xi = ar * br - ai * bi, ar * bi + ai * br
        yr, yi = xr * cr - xi * ci, xr * ci + xi * cr
        if first:
            lane = iota((block, 128), 1) == 0
            yr = jnp.where(lane, ar * br * cr, yr)
            yi = jnp.where(lane, ai * bi * ci, yi)
        p_ref[r, 0:128] = yr.astype(BF)
        p_ref[r, 128:256] = yi.astype(BF)


def real_sixteen(y0, y8, re, im):
    h, C, S = (jnp.float32(v) for v in (math.sqrt(0.5), math.cos(math.pi / 8), math.sin(math.pi / 8)))
    a, b = y0 + y8, y0 - y8
    r4, i4 = re(4), im(4)
    ee = [a + r4, b - i4, a - r4, b + i4]
    r2, i2, r6, i6 = re(2), im(2), re(6), im(6)
    d, e = h * (r2 - r6), h * (i2 + i6)
    eo = [r2 + r6, d - e, i6 - i2, -d - e]
    even = [ee[q] + eo[q] for q in range(4)] + [ee[q] - eo[q] for q in range(4)]
    r1, r7, i1, i7 = re(1), re(7), im(1), im(7)
    r3, r5, i3, i5 = re(3), re(5), im(3), im(5)
    p1, m1, q1, n1 = r1 + r7, r1 - r7, i1 - i7, i1 + i7
    p3, m3, q3, n3 = r3 + r5, r3 - r5, i3 - i5, i3 + i5
    dp, dq = h * (p1 - p3), h * (q1 + q3)
    u1, v1 = m1 * C + m3 * S, n1 * S + n3 * C
    u3, v3 = m1 * S - m3 * C, n1 * C - n3 * S
    odd = [p1 + p3, u1 - v1, dp - dq, u3 - v3, q3 - q1, -u3 - v3, -dp - dq, -u1 - v1]
    return [even[q] + odd[q] for q in range(8)] + [even[q] - odd[q] for q in range(8)]


def combine_even(start, stop, y_ref):
    for n in range(start, stop):
        r = slice(8 * n, 8 * n + 8)
        out = real_sixteen(y_ref[0, r, 0:128], y_ref[0, r, 128:256],
                           lambda g: y_ref[g, r, 0:128], lambda g: y_ref[g, r, 128:256])
        for q in range(16):
            y_ref[q // 2, r, 128 * (q % 2):128 * (q % 2) + 128] = out[q]


def combine_odd(rows, y_ref, f_ref):
    block = 16
    cos = lambda n: jnp.float32(math.cos(math.pi * n / 16))
    sin = lambda n: jnp.float32(math.sin(math.pi * n / 16))
    h, C, S = (jnp.float32(v) for v in (math.sqrt(0.5), math.cos(math.pi / 8), math.sin(math.pi / 8)))

    def put(r, q, value, f_ref):
        lanes = slice(128 * (q % 2), 128 * (q % 2) + 128)
        even = y_ref[q // 2, r, lanes]
        f_ref[q // 2, r, lanes] = (even + value).astype(BF)
        f_ref[8 + q // 2, r, lanes] = (even - value).astype(BF)

    def parts(r, sign):
        re = lambda g: y_ref[8 + g // 2, r, 0:128]
        im = lambda g: y_ref[8 + g // 2, r, 128:256]
        a = {g: re(g) + re(16 - g) if sign > 0 else re(g) - re(16 - g) for g in (1, 3, 5, 7)}
        b = {g: im(g) - im(16 - g) if sign > 0 else im(g) + im(16 - g) for g in (1, 3, 5, 7)}
        return a, b

    def evens(n, carry):
        r = pl.ds(pl.multiple_of(n * block, block), block)
        p, q = parts(r, 1)
        p1, m1, q1, n1 = p[1] + p[7], p[1] - p[7], q[1] - q[7], q[1] + q[7]
        p3, m3, q3, n3 = p[3] + p[5], p[3] - p[5], q[3] - q[5], q[3] + q[5]
        put(r, 0, p1 + p3, f_ref)
        put(r, 8, q3 - q1, f_ref)
        dp, dq = h * (p1 - p3), h * (q1 + q3)
        put(r, 4, dp - dq, f_ref)
        put(r, 12, -dp - dq, f_ref)
        u1, v1 = m1 * C + m3 * S, n1 * S + n3 * C
        put(r, 2, u1 - v1, f_ref)
        put(r, 14, -u1 - v1, f_ref)
        u3, v3 = m1 * S - m3 * C, n1 * C - n3 * S
        put(r, 6, u3 - v3, f_ref)
        put(r, 10, -u3 - v3, f_ref)
        return carry

    def odds(n, carry):
        r = pl.ds(pl.multiple_of(n * block, block), block)
        m, w = parts(r, -1)
        for c in (1, 3, 5, 7):
            u = m[1] * cos(c) + m[3] * cos(3 * c) + m[5] * cos(5 * c) + m[7] * cos(7 * c)
            v = w[1] * sin(c) + w[3] * sin(3 * c) + w[5] * sin(5 * c) + w[7] * sin(7 * c)
            put(r, c, u - v, f_ref)
            put(r, 16 - c, -u - v, f_ref)
        return carry

    lax.fori_loop(0, rows // block, evens, 0, unroll=2)
    lax.fori_loop(0, rows // block, odds, 0, unroll=2)


def sketch(rows, load_rows, bid_ref, sign_ref, x2, cube, e_ref, step_ref, base_ref, ta, tb, wa, wb, sa, sb, pa, pb,
           y_ref, f_ref):
    inverse_first(base_ref, wa)
    for k in range(3):
        table_first(k, bid_ref, sign_ref, e_ref, step_ref, ta)
        if k == 0:
            load_rows()
        sa[:, 256 * k:256 * k + 256] = spectrum(x2, ta, k)
    groups = EVEN + ODD
    slots = [0] + [g // 2 + 8 * (g % 2) for g in groups]
    for k in range(3):
        table_next(k, groups[0], e_ref, step_ref, tb)
    inverse_next(groups[0], base_ref, wb)
    bufs = ((ta, wa, sa, pa), (tb, wb, sb, pb))
    blocks = rows // 8
    for n in range(1, 16):
        t, w, s, p = bufs[n % 2]
        t_old, w_old, s_old, p_old = bufs[(n + 1) % 2]
        for k in range(3):
            s[:, 256 * k:256 * k + 256] = spectrum(x2, t, k)
        multiply(rows, n == 1, s_old, cube, p_old)
        if n < 15:
            g = groups[n]
            for k in range(3):
                table_next(k, g, e_ref, step_ref, t_old)
        y_ref[slots[n - 1]] = dot(p_old[...], w_old[...])
        if n < 15:
            inverse_next(g, base_ref, w_old)
        if n >= 9 and n < 15:
            combine_even(blocks * (n - 9) // 6, blocks * (n - 8) // 6, y_ref)
    multiply(rows, False, sb, cube, pb)
    y_ref[slots[15]] = dot(pb[...], wb[...])
    combine_odd(rows, y_ref, f_ref)


def scratch(rows):
    return [
        pltpu.VMEM((rows, 512), BF),
        pltpu.VMEM((rows, 128), F32),
        pltpu.VMEM((3, 2, 256, 128), F32),
        pltpu.VMEM((3, 2, 256, 128), F32),
        pltpu.VMEM((2, 128, 128), F32),
        pltpu.VMEM((512, 768), BF),
        pltpu.VMEM((512, 768), BF),
        pltpu.VMEM((256, 256), BF),
        pltpu.VMEM((256, 256), BF),
        pltpu.VMEM((rows, 768), F32),
        pltpu.VMEM((rows, 768), F32),
        pltpu.VMEM((rows, 256), BF),
        pltpu.VMEM((rows, 256), BF),
        pltpu.VMEM((16, rows, 256), F32),
        pltpu.VMEM((16, rows, 256), BF),
    ]


MESH = pl.DeviceIdType.MESH


def fused_kernel(rows, x_hbm, target_hbm, count_hbm, bid_hbm, sign_hbm, gram_ref, zty_ref,
                 x_ref, target_ref, count_ref, bid_ref, sign_ref, in_sem, *refs):
    inputs = [pltpu.make_async_copy(src, dst, in_sem.at[i]) for i, (src, dst) in enumerate((
        (bid_hbm, bid_ref), (sign_hbm, sign_ref), (count_hbm, count_ref), (x_hbm, x_ref), (target_hbm, target_ref)))]
    for copy in inputs:
        copy.start()
    (half, mine, sib, tx, rx, ry, zown, sibz, zpair, zx, zall,
     sib_send, sib_recv, send, recv, z_send, z_recv) = refs[-17:]
    x2, cube, f_ref = refs[0], refs[1], refs[-18]
    d = lax.axis_index("dp")
    core, lane, turn = d % 2, (d // 2) % 2, d // 4

    def device(turns, other):
        return 4 * ((turn + turns) % 4) + 2 * ((lane + other) % 2) + core

    def choose(first, second):
        return first * (1 - core) + second * core

    sibling = d + 1 - 2 * core
    across, one, two, three = device(0, 1), device(1, 0), device(2, 0), device(3, 0)
    neighbours = (sibling, across, one, two, three)
    barrier = pltpu.get_barrier_semaphore()
    for peer in neighbours:
        pl.semaphore_signal(barrier, inc=1, device_id={"dp": peer}, device_id_type=MESH)

    def remote(src, dst, send_sem, recv_sem, peer):
        return pltpu.make_async_remote_copy(
            src_ref=src, dst_ref=dst, send_sem=send_sem, recv_sem=recv_sem,
            device_id={"dp": peer}, device_id_type=MESH)

    def load_rows():
        for copy in inputs[2:]:
            copy.wait()
        live = count_ref[d]
        xf = jnp.where(iota((rows, 256), 0) < live, x_ref[...].astype(F32), 0.0)
        s = lax.rsqrt(jnp.mean(xf * xf, axis=1, keepdims=True) + 1e-6) * (1.0 / 16)
        cube[...] = jnp.broadcast_to(s * s * s, (rows, 128))
        x2[:, 0:256] = xf.astype(BF)
        x2[:, 256:512] = xf.astype(BF)

    for copy in inputs[:2]:
        copy.wait()
    sketch(rows, load_rows, bid_ref, sign_ref, *refs[:-17])

    own = f_ref[lax.axis_index("feat")]
    target = jnp.concatenate(
        [jnp.broadcast_to(target_ref[n:n + 1, :].astype(F32), (8, 128)) for n in range(rows // 128)],
        axis=1).astype(BF)
    zown[...] = dot(target, own)
    turned = own.astype(F32).T.astype(BF)
    pl.semaphore_wait(barrier, len(neighbours))

    lanes_first = ((2, 1), (1, 1), (3, 1), (0, 1), (2, 0), (1, 0), (3, 0), (0, 0))
    rings_first = ((2, 1), (2, 0), (1, 1), (3, 1), (1, 0), (3, 0), (0, 1), (0, 0))
    zero_chip = [(device(*at) - core) for at in lanes_first]
    one_chip = [(device(*at) - core) for at in rings_first]
    pair = [remote(half.at[i], sib.at[i], sib_send.at[i], sib_recv.at[i], sibling) for i in range(8)]
    low, high = slice(0, 128), slice(128, 256)

    def ring(base, relay, far, near, back, at_near, at_back):
        def one_copy(i, src, dst, part, peer):
            return remote(src.at[part], dst.at[part], send.at[base + i], recv.at[base + i], peer)
        return [one_copy(0, tx.at[far], ry.at[relay], low, one), one_copy(1, tx.at[far], ry.at[relay], high, three),
                one_copy(2, tx.at[near], rx.at[at_near], high, one), one_copy(3, tx.at[back], rx.at[at_back], low, three),
                one_copy(4, tx.at[near], rx.at[at_near], low, one), one_copy(5, tx.at[back], rx.at[at_back], high, three)]

    cross = [remote(tx.at[i], rx.at[i], send.at[i], recv.at[i], across) for i in range(4)]
    late = ring(4, 0, 4, 5, 6, 4, 5)
    early = [ring(0, 0, 0, 2, 3, 0, 1), ring(6, 1, 1, 4, 5, 2, 3)]
    last = remote(tx.at[6], rx.at[6], send.at[12], recv.at[12], across)
    z_pair = remote(zown, sibz, z_send.at[0], z_recv.at[0], sibling)
    z_lane = remote(zpair, zx, z_send.at[1], z_recv.at[1], across)
    z_ring = [remote(zall.at[turn], zall.at[turn], z_send.at[2 + i], z_recv.at[2 + i], peer)
              for i, peer in enumerate((one, two, three))]

    def finish(k):
        pair[k].wait_recv()
        total = mine[k] + sib[k].astype(F32)
        if k < 6:
            tx[k] = total.astype(BF)
        if k > 1:
            mine[k] = total

    def begin(k):
        if k < 4:
            @pl.when(core == 0)
            def _():
                cross[k].start()
        if k < 6:
            @pl.when(core == 1)
            def _():
                for copy in (early[k][0:2] if k < 2 else early[(k - 2) // 2][2 + k % 2:3 + k % 2]):
                    copy.start()

    for i in range(8):
        half[i] = dot(turned, f_ref[choose(one_chip[i] + 1, zero_chip[i])]).astype(BF)
        if i == 0:
            z_pair.start()
        if i >= 2:
            begin(i - 2)
        mine[i] = dot(turned, f_ref[choose(zero_chip[i], one_chip[i] + 1)])
        pair[i].start()
        if i >= 1:
            finish(i - 1)
        if i == 3:
            z_pair.wait_recv()
            zpair[...] = zown[...] + sibz[...]
        if i == 4:
            z_lane.start()
    finish(7)

    def add_relays(copies, relay, near, back):
        copies[0].wait_recv()
        tx[near, low] = (mine[near, low] + ry[relay, low].astype(F32)).astype(BF)
        copies[1].wait_recv()
        tx[back, high] = (mine[back, high] + ry[relay, high].astype(F32)).astype(BF)
        copies[4].start()
        copies[5].start()

    @pl.when(core == 0)
    def _():
        for k in range(3):
            cross[k].wait_recv()
            total = mine[4 + k] + rx[k].astype(F32)
            tx[4 + k] = total.astype(BF)
            if k > 0:
                mine[4 + k] = total
            if k == 1:
                late[0].start()
                late[1].start()
            if k == 2:
                late[2].start()
        late[3].start()
        add_relays(late, 0, 5, 6)
        cross[3].wait_recv()
        mine[7] = mine[7] + rx[3].astype(F32)

    @pl.when(core == 1)
    def _():
        add_relays(early[0], 0, 2, 3)
        add_relays(early[1], 1, 4, 5)
        for copy in early[0][2:6]:
            copy.wait_recv()
        tx[6] = (mine[6] + rx[0].astype(F32) + rx[1].astype(F32)).astype(BF)
        for copy in early[1][2:4]:
            copy.wait_recv()
        last.start()

    z_lane.wait_recv()
    zall[turn] = zpair[...] + zx[...]

    @pl.when(core == 0)
    def _():
        for copy in z_ring:
            copy.start()
        for copy in late[2:6]:
            copy.wait_recv()
        mine[0] = mine[7] + rx[4].astype(F32) + rx[5].astype(F32)
        for copy in cross + late:
            copy.wait_send()

    @pl.when(core == 1)
    def _():
        for copy in z_ring:
            copy.start()
        for copy in early[1][4:6]:
            copy.wait_recv()
        total = mine[7] + rx[2].astype(F32) + rx[3].astype(F32)
        last.wait_recv()
        mine[0] = total + rx[6].astype(F32)
        for copy in early[0] + early[1] + [last]:
            copy.wait_send()

    for copy in z_ring:
        copy.wait_recv()
    zty_ref[...] = ((zall[0] + zall[1]) + (zall[2] + zall[3]))[0:1] * jnp.float32(6144 ** -0.5)
    gram_ref[...] = mine[0].T * jnp.float32(1.0 / 6144)
    for copy in pair + [z_pair, z_lane] + z_ring:
        copy.wait_send()


def fused_call(rows):
    vmem = pl.BlockSpec(memory_space=pltpu.VMEM)
    dma = pltpu.SemaphoreType.DMA
    return pl.pallas_call(
        functools.partial(fused_kernel, rows),
        out_shape=(jax.ShapeDtypeStruct((256, 256), F32), jax.ShapeDtypeStruct((1, 256), F32)),
        in_specs=[pl.BlockSpec(memory_space=pltpu.HBM)] * 5,
        out_specs=[vmem, vmem],
        scratch_shapes=[
            pltpu.VMEM((rows, 256), BF),
            pltpu.VMEM((rows // 128, 128), BF),
            pltpu.SMEM((16,), I32),
            pltpu.VMEM((3, 256), I32),
            pltpu.VMEM((3, 256), I32),
            dma((5,)),
        ] + scratch(rows) + [
            pltpu.VMEM((8, 256, 256), BF),
            pltpu.VMEM((8, 256, 256), F32),
            pltpu.VMEM((8, 256, 256), BF),
            pltpu.VMEM((7, 256, 256), BF),
            pltpu.VMEM((7, 256, 256), BF),
            pltpu.VMEM((2, 256, 256), BF),
            pltpu.VMEM((8, 256), F32),
            pltpu.VMEM((8, 256), F32),
            pltpu.VMEM((8, 256), F32),
            pltpu.VMEM((8, 256), F32),
            pltpu.VMEM((4, 8, 256), F32),
            dma((8,)), dma((8,)), dma((13,)), dma((13,)), dma((5,)), dma((5,)),
        ],
        compiler_params=pltpu.CompilerParams(
            collective_id=0, has_side_effects=True, vmem_limit_bytes=46 << 20),
        name="fused",
    )


def body(samples, targets, counts, bucket_ids, sign_bits):
    rows = samples.shape[0]
    operands = (samples, targets.reshape(rows // 128, 128), counts, bucket_ids, sign_bits)
    gram, zty = fused_call(rows)(
        *[pltpu.with_memory_space_constraint(value, pltpu.HBM) for value in operands])
    return gram, zty.reshape(256)


def solution(mesh):
    placed = (P("dp", None), P("dp"), P(), P(), P())
    return jax.shard_map(
        body, mesh=mesh, in_specs=placed, out_specs=(P("dp", "feat"), P("feat")), check_vma=False
    )
```

```python
import functools, math
import jax, jax.numpy as jnp
from jax import lax
from jax.experimental import pallas as pl
from jax.experimental.pallas import tpu as pltpu
from jax.sharding import PartitionSpec as P

F32, BF, I32 = jnp.float32, jnp.bfloat16, jnp.int32
SK = 4096
SPLIT = 2


def sin_poly(t):
    u = t * t
    p = jnp.float32(2.6019031e-06)
    p = p * u + jnp.float32(-1.9807414e-04)
    p = p * u + jnp.float32(8.3330255e-03)
    p = p * u + jnp.float32(-1.6666657e-01)
    return t + t * (u * p)


def sin_turn(n, period):
    quarter = period // 4
    m = ((n + quarter) & (period - 1)) - quarter
    m = jnp.where(m > quarter, period // 2 - m, m)
    return sin_poly(m.astype(F32) * jnp.float32(2.0 * math.pi / period))


def cos_turn(n, period):
    return sin_turn(n + period // 4, period)


def iota(shape, dim):
    return lax.broadcasted_iota(I32, shape, dim)


def dot(a, b):
    return jnp.dot(a, b, preferred_element_type=F32)


EVEN, ODD = (2, 4, 6, 8, 10, 12, 14), (1, 3, 5, 7, 9, 11, 13, 15)


def column(k, bid_ref, sign_ref):
    packed = bid_ref[k:k + 1, :] + SK * sign_ref[k:k + 1, :]
    eye = iota((256, 256), 0) == iota((256, 256), 1)
    both = jnp.sum(jnp.where(eye, packed.astype(F32), 0.0), axis=1, keepdims=True)
    both = jnp.broadcast_to(both, (256, 128)).astype(I32)
    return both & (SK - 1), (2 * (both >> 12) - 1).astype(F32)


def put_split(t_ref, k, part, value):
    col = 256 * k + 128 * part
    hi = value.astype(BF)
    t_ref[0:256, col:col + 128] = hi
    if k < SPLIT:
        t_ref[256:512, col:col + 128] = (value - hi.astype(F32)).astype(BF)


def spectrum(x2, t_ref, k):
    lanes = slice(256 * k, 256 * k + 256)
    depth = 512 if k < SPLIT else 256
    return dot(x2[:, 0:depth], t_ref[0:depth, lanes])


def table_first(k, bid_ref, sign_ref, e_ref, step_ref, t_ref):
    b, s = column(k, bid_ref, sign_ref)
    lane = iota((256, 128), 1)
    er, ei = s * cos_turn(b * lane, 128), -s * sin_turn(b * lane, 128)
    e_ref[k, 0] = er
    e_ref[k, 1] = ei
    sr, si = cos_turn(b * lane, SK), -sin_turn(b * lane, SK)
    step_ref[k, 0] = sr
    step_ref[k, 1] = si
    flip = (1 - 2 * (b & 1)).astype(F32)
    hr, hi = flip * sr[:, 16:17], flip * si[:, 16:17]
    low = lane < 64
    put_split(t_ref, k, 0, jnp.where(low, er, er * hr - ei * hi))
    put_split(t_ref, k, 1, jnp.where(lane == 0, s * flip, jnp.where(low, ei, er * hi + ei * hr)))


def table_next(k, g, e_ref, step_ref, t_ref):
    sr, si = step_ref[k, 0, :, g:g + 1], step_ref[k, 1, :, g:g + 1]
    er, ei = e_ref[k, 0], e_ref[k, 1]
    put_split(t_ref, k, 0, er * sr - ei * si)
    put_split(t_ref, k, 1, er * si + ei * sr)


def inverse_first(base_ref, w_ref):
    n = iota((128, 128), 0) * iota((128, 128), 1)
    base_ref[0] = cos_turn(n, 128)
    base_ref[1] = sin_turn(n, 128)
    row = iota((128, 128), 0)
    c2 = iota((128, 128), 1)
    low = row < 64
    f = jnp.where(low, 32 * row, 16 + 32 * (row - 64))
    gain = jnp.where(row == 0, 1.0 / 64, 2.0 / 64)
    wr = cos_turn(f * c2, SK) * gain
    wi = sin_turn(f * c2, SK) * (-2.0 / 64)
    wi = jnp.where(row == 0, (1 - 2 * (c2 & 1)).astype(F32) * (1.0 / 64), wi)
    for at, w in ((0, wr), (128, wi)):
        w_ref[at:at + 128, 0:128] = jnp.where(low, w, 0.0).astype(BF)
        w_ref[at:at + 128, 128:256] = jnp.where(low, 0.0, w).astype(BF)


def inverse_next(g, base_ref, w_ref):
    c2 = iota((8, 128), 1)
    r, i = cos_turn(g * c2, SK)[0:1] * (2.0 / 64), sin_turn(g * c2, SK)[0:1] * (2.0 / 64)
    c, s = base_ref[0], base_ref[1]
    wr, wi = c * r - s * i, s * r + c * i
    w_ref[0:128, 0:128] = wr.astype(BF)
    w_ref[0:128, 128:256] = wi.astype(BF)
    w_ref[128:256, 0:128] = (-wi).astype(BF)
    w_ref[128:256, 128:256] = wr.astype(BF)


def multiply(rows, first, spec_ref, cube_ref, p_ref):
    block = 16
    for n in range(rows // block):
        r = slice(block * n, block * n + block)
        cube = cube_ref[r, :]
        ar, ai, br, bi, cr, ci = [spec_ref[r, 128 * q:128 * q + 128] for q in range(6)]
        ar, ai = ar * cube, ai * cube
        xr, xi = ar * br - ai * bi, ar * bi + ai * br
        yr, yi = xr * cr - xi * ci, xr * ci + xi * cr
        if first:
            lane = iota((block, 128), 1) == 0
            yr = jnp.where(lane, ar * br * cr, yr)
            yi = jnp.where(lane, ai * bi * ci, yi)
        p_ref[r, 0:128] = yr.astype(BF)
        p_ref[r, 128:256] = yi.astype(BF)


def real_sixteen(y0, y8, re, im):
    h, C, S = (jnp.float32(v) for v in (math.sqrt(0.5), math.cos(math.pi / 8), math.sin(math.pi / 8)))
    a, b = y0 + y8, y0 - y8
    r4, i4 = re(4), im(4)
    ee = [a + r4, b - i4, a - r4, b + i4]
    r2, i2, r6, i6 = re(2), im(2), re(6), im(6)
    d, e = h * (r2 - r6), h * (i2 + i6)
    eo = [r2 + r6, d - e, i6 - i2, -d - e]
    even = [ee[q] + eo[q] for q in range(4)] + [ee[q] - eo[q] for q in range(4)]
    r1, r7, i1, i7 = re(1), re(7), im(1), im(7)
    r3, r5, i3, i5 = re(3), re(5), im(3), im(5)
    p1, m1, q1, n1 = r1 + r7, r1 - r7, i1 - i7, i1 + i7
    p3, m3, q3, n3 = r3 + r5, r3 - r5, i3 - i5, i3 + i5
    dp, dq = h * (p1 - p3), h * (q1 + q3)
    u1, v1 = m1 * C + m3 * S, n1 * S + n3 * C
    u3, v3 = m1 * S - m3 * C, n1 * C - n3 * S
    odd = [p1 + p3, u1 - v1, dp - dq, u3 - v3, q3 - q1, -u3 - v3, -dp - dq, -u1 - v1]
    return [even[q] + odd[q] for q in range(8)] + [even[q] - odd[q] for q in range(8)]


def combine_even(start, stop, y_ref):
    for n in range(start, stop):
        r = slice(8 * n, 8 * n + 8)
        out = real_sixteen(y_ref[0, r, 0:128], y_ref[0, r, 128:256],
                           lambda g: y_ref[g, r, 0:128], lambda g: y_ref[g, r, 128:256])
        for q in range(16):
            y_ref[q // 2, r, 128 * (q % 2):128 * (q % 2) + 128] = out[q]


def combine_odd(rows, y_ref, f_ref):
    block = 16
    cos = lambda n: jnp.float32(math.cos(math.pi * n / 16))
    sin = lambda n: jnp.float32(math.sin(math.pi * n / 16))
    h, C, S = (jnp.float32(v) for v in (math.sqrt(0.5), math.cos(math.pi / 8), math.sin(math.pi / 8)))

    def put(r, q, value, f_ref, negated=False):
        lanes = slice(128 * (q % 2), 128 * (q % 2) + 128)
        even = y_ref[q // 2, r, lanes]
        plus, minus = (8, 0) if negated else (0, 8)
        f_ref[plus + q // 2, r, lanes] = (even + value).astype(BF)
        f_ref[minus + q // 2, r, lanes] = (even - value).astype(BF)

    def parts(r, sign):
        re = lambda g: y_ref[8 + g // 2, r, 0:128]
        im = lambda g: y_ref[8 + g // 2, r, 128:256]
        a = {g: re(g) + re(16 - g) if sign > 0 else re(g) - re(16 - g) for g in (1, 3, 5, 7)}
        b = {g: im(g) - im(16 - g) if sign > 0 else im(g) + im(16 - g) for g in (1, 3, 5, 7)}
        return a, b

    def evens(n, carry):
        r = pl.ds(pl.multiple_of(n * block, block), block)
        p, q = parts(r, 1)
        p1, m1, q1, n1 = p[1] + p[7], p[1] - p[7], q[1] - q[7], q[1] + q[7]
        p3, m3, q3, n3 = p[3] + p[5], p[3] - p[5], q[3] - q[5], q[3] + q[5]
        put(r, 0, p1 + p3, f_ref)
        put(r, 8, q3 - q1, f_ref)
        dp, dq = h * (p1 - p3), h * (q1 + q3)
        put(r, 4, dp - dq, f_ref)
        put(r, 12, dp + dq, f_ref, True)
        u1, v1 = m1 * C + m3 * S, n1 * S + n3 * C
        put(r, 2, u1 - v1, f_ref)
        put(r, 14, u1 + v1, f_ref, True)
        u3, v3 = m1 * S - m3 * C, n1 * C - n3 * S
        put(r, 6, u3 - v3, f_ref)
        put(r, 10, u3 + v3, f_ref, True)
        return carry

    def odds(n, carry):
        r = pl.ds(pl.multiple_of(n * block, block), block)
        m, w = parts(r, -1)
        for c in (1, 3, 5, 7):
            u = m[1] * cos(c) + m[3] * cos(3 * c) + m[5] * cos(5 * c) + m[7] * cos(7 * c)
            v = w[1] * sin(c) + w[3] * sin(3 * c) + w[5] * sin(5 * c) + w[7] * sin(7 * c)
            put(r, c, u - v, f_ref)
            put(r, 16 - c, u + v, f_ref, True)
        return carry

    lax.fori_loop(0, rows // block, evens, 0, unroll=2)
    lax.fori_loop(0, rows // block, odds, 0, unroll=2)


def sketch(rows, load_rows, bid_ref, sign_ref, x2, cube, e_ref, step_ref, base_ref, ta, tb, wa, wb, sa, sb, pa, pb,
           y_ref, f_ref):
    inverse_first(base_ref, wa)
    for k in range(3):
        table_first(k, bid_ref, sign_ref, e_ref, step_ref, ta)
        if k == 0:
            load_rows()
        sa[:, 256 * k:256 * k + 256] = spectrum(x2, ta, k)
    groups = EVEN + ODD
    slots = [0] + [g // 2 + 8 * (g % 2) for g in groups]
    for k in range(3):
        table_next(k, groups[0], e_ref, step_ref, tb)
    inverse_next(groups[0], base_ref, wb)
    bufs = ((ta, wa, sa, pa), (tb, wb, sb, pb))
    blocks = rows // 8
    for n in range(1, 16):
        t, w, s, p = bufs[n % 2]
        t_old, w_old, s_old, p_old = bufs[(n + 1) % 2]
        for k in range(3):
            s[:, 256 * k:256 * k + 256] = spectrum(x2, t, k)
        multiply(rows, n == 1, s_old, cube, p_old)
        if n < 15:
            g = groups[n]
            for k in range(3):
                table_next(k, g, e_ref, step_ref, t_old)
        y_ref[slots[n - 1]] = dot(p_old[...], w_old[...])
        if n < 15:
            inverse_next(g, base_ref, w_old)
        if n >= 9 and n < 15:
            combine_even(blocks * (n - 9) // 6, blocks * (n - 8) // 6, y_ref)
    multiply(rows, False, sb, cube, pb)
    y_ref[slots[15]] = dot(pb[...], wb[...])
    combine_odd(rows, y_ref, f_ref)


def scratch(rows):
    return [
        pltpu.VMEM((rows, 512), BF),
        pltpu.VMEM((rows, 128), F32),
        pltpu.VMEM((3, 2, 256, 128), F32),
        pltpu.VMEM((3, 2, 256, 128), F32),
        pltpu.VMEM((2, 128, 128), F32),
        pltpu.VMEM((512, 768), BF),
        pltpu.VMEM((512, 768), BF),
        pltpu.VMEM((256, 256), BF),
        pltpu.VMEM((256, 256), BF),
        pltpu.VMEM((rows, 768), F32),
        pltpu.VMEM((rows, 768), F32),
        pltpu.VMEM((rows, 256), BF),
        pltpu.VMEM((rows, 256), BF),
        pltpu.VMEM((16, rows, 256), F32),
        pltpu.VMEM((16, rows, 256), BF),
    ]


MESH = pl.DeviceIdType.MESH


def fused_kernel(rows, x_hbm, target_hbm, count_hbm, bid_hbm, sign_hbm, gram_ref, zty_ref,
                 x_ref, target_ref, count_ref, bid_ref, sign_ref, in_sem, *refs):
    inputs = [pltpu.make_async_copy(src, dst, in_sem.at[i]) for i, (src, dst) in enumerate((
        (bid_hbm, bid_ref), (sign_hbm, sign_ref), (count_hbm, count_ref), (x_hbm, x_ref), (target_hbm, target_ref)))]
    for copy in inputs:
        copy.start()
    (half, mine, sib, tx, rx, zown, sibz, zpair, zx, zall,
     sib_send, sib_recv, send, recv, z_send, z_recv) = refs[-16:]
    x2, cube, f_ref = refs[0], refs[1], refs[-17]
    d = lax.axis_index("dp")
    core, lane, ring = d % 2, (d // 2) % 2, d // 4

    def device(turn, other):
        return 4 * ((ring + turn) % 4) + 2 * ((lane + other) % 2) + core

    def choose(first, second):
        return first * (1 - core) + second * core

    sibling = d + 1 - 2 * core
    across, one, two, three = device(0, 1), device(1, 0), device(2, 0), device(3, 0)
    neighbours = (sibling, across, one, two, three)
    barrier = pltpu.get_barrier_semaphore()
    for peer in neighbours:
        pl.semaphore_signal(barrier, inc=1, device_id={"dp": peer}, device_id_type=MESH)

    def remote(src, dst, send_sem, recv_sem, peer):
        return pltpu.make_async_remote_copy(
            src_ref=src, dst_ref=dst, send_sem=send_sem, recv_sem=recv_sem,
            device_id={"dp": peer}, device_id_type=MESH)

    def load_rows():
        for copy in inputs[2:]:
            copy.wait()
        live = count_ref[d]
        xf = jnp.where(iota((rows, 256), 0) < live, x_ref[...].astype(F32), 0.0)
        s = lax.rsqrt(jnp.mean(xf * xf, axis=1, keepdims=True) + 1e-6) * (1.0 / 16)
        cube[...] = jnp.broadcast_to(s * s * s, (rows, 128))
        x2[:, 0:256] = xf.astype(BF)
        x2[:, 256:512] = xf.astype(BF)

    for copy in inputs[:2]:
        copy.wait()
    sketch(rows, load_rows, bid_ref, sign_ref, *refs[:-16])

    own = f_ref[lax.axis_index("feat")]
    target = jnp.concatenate(
        [jnp.broadcast_to(target_ref[n:n + 1, :].astype(F32), (8, 128)) for n in range(rows // 128)],
        axis=1).astype(BF)
    zown[...] = dot(target, own)
    turned = own.astype(F32).T.astype(BF)
    pl.semaphore_wait(barrier, len(neighbours))

    lanes_first = ((2, 1), (1, 1), (3, 1), (0, 1), (2, 0), (1, 0), (3, 0), (0, 0))
    rings_first = ((2, 1), (1, 1), (3, 1), (2, 0), (1, 0), (3, 0), (0, 1), (0, 0))
    zero_chip = [(device(*at) - core) for at in lanes_first]
    one_chip = [(device(*at) - core) for at in rings_first]
    peers = [choose(a, b) for a, b in zip(
        (across, across, across, across, two, one, three), (two, one, three, two, one, three, across))]
    pair = [remote(half.at[i], sib.at[i], sib_send.at[i], sib_recv.at[i], sibling) for i in range(8)]
    message = [remote(tx.at[i], rx.at[i], send.at[i], recv.at[i], peers[i]) for i in range(7)]
    z_pair = remote(zown, sibz, z_send.at[0], z_recv.at[0], sibling)
    z_lane = remote(zpair, zx, z_send.at[1], z_recv.at[1], across)
    z_ring = [remote(zall.at[ring], zall.at[ring], z_send.at[2 + i], z_recv.at[2 + i], peer)
              for i, peer in enumerate((one, two, three))]

    def finish(k):
        pair[k].wait_recv()
        total = mine[k] + sib[k].astype(F32)
        if k < 6:
            tx[k] = total.astype(BF)
        if k > 3:
            mine[k] = total

    def begin(k):
        if k < 4:
            message[k].start()
        elif k < 6:
            @pl.when(core == 1)
            def _():
                message[k].start()

    for i in range(8):
        half[i] = dot(turned, f_ref[choose(one_chip[i] + 1, zero_chip[i])]).astype(BF)
        if i == 0:
            z_pair.start()
        if i >= 4:
            begin(i - 4)
        mine[i] = dot(turned, f_ref[choose(zero_chip[i], one_chip[i] + 1)])
        pair[i].start()
        if i >= 3:
            finish(i - 3)
        if i == 3:
            z_pair.wait_recv()
            zpair[...] = zown[...] + sibz[...]
        if i == 4:
            z_lane.start()
    finish(5)
    begin(4)
    finish(6)
    begin(5)
    finish(7)

    @pl.when(core == 0)
    def _():
        for k in range(3):
            message[k].wait_recv()
            tx[4 + k] = (mine[4 + k] + rx[k].astype(F32)).astype(BF)
            if k > 0:
                message[3 + k].start()
        message[3].wait_recv()
        mine[0] = mine[7] + rx[3].astype(F32)
        message[6].start()

    @pl.when(core == 1)
    def _():
        for k in (0, 1, 2):
            message[k].wait_recv()
        tx[6] = (mine[6] + rx[0].astype(F32) + rx[1].astype(F32) + rx[2].astype(F32)).astype(BF)
        message[3].wait_recv()
        mine[0] = mine[7] + rx[3].astype(F32)
        message[6].start()

    z_lane.wait_recv()
    zall[ring] = zpair[...] + zx[...]

    @pl.when(core == 0)
    def _():
        for copy in z_ring:
            copy.start()
        message[4].wait_recv()
        message[5].wait_recv()
        mine[0] = mine[0] + rx[4].astype(F32) + rx[5].astype(F32)

    @pl.when(core == 1)
    def _():
        for copy in z_ring:
            copy.start()
        message[4].wait_recv()
        message[5].wait_recv()
        mine[0] = mine[0] + rx[4].astype(F32) + rx[5].astype(F32)

    for copy in z_ring:
        copy.wait_recv()
    zty_ref[...] = ((zall[0] + zall[1]) + (zall[2] + zall[3]))[0:1] * jnp.float32(6144 ** -0.5)
    message[6].wait_recv()
    gram_ref[...] = (mine[0] + rx[6].astype(F32)).T * jnp.float32(1.0 / 6144)
    for copy in pair + message + [z_pair, z_lane] + z_ring:
        copy.wait_send()


def fused_call(rows):
    vmem = pl.BlockSpec(memory_space=pltpu.VMEM)
    dma = pltpu.SemaphoreType.DMA
    return pl.pallas_call(
        functools.partial(fused_kernel, rows),
        out_shape=(jax.ShapeDtypeStruct((256, 256), F32), jax.ShapeDtypeStruct((1, 256), F32)),
        in_specs=[pl.BlockSpec(memory_space=pltpu.HBM)] * 5,
        out_specs=[vmem, vmem],
        scratch_shapes=[
            pltpu.VMEM((rows, 256), BF),
            pltpu.VMEM((rows // 128, 128), BF),
            pltpu.SMEM((16,), I32),
            pltpu.VMEM((3, 256), I32),
            pltpu.VMEM((3, 256), I32),
            dma((5,)),
        ] + scratch(rows) + [
            pltpu.VMEM((8, 256, 256), BF),
            pltpu.VMEM((8, 256, 256), F32),
            pltpu.VMEM((8, 256, 256), BF),
            pltpu.VMEM((7, 256, 256), BF),
            pltpu.VMEM((7, 256, 256), BF),
            pltpu.VMEM((8, 256), F32),
            pltpu.VMEM((8, 256), F32),
            pltpu.VMEM((8, 256), F32),
            pltpu.VMEM((8, 256), F32),
            pltpu.VMEM((4, 8, 256), F32),
            dma((8,)), dma((8,)), dma((7,)), dma((7,)), dma((5,)), dma((5,)),
        ],
        compiler_params=pltpu.CompilerParams(
            collective_id=0, has_side_effects=True, vmem_limit_bytes=46 << 20),
        name="fused",
    )


def body(samples, targets, counts, bucket_ids, sign_bits):
    rows = samples.shape[0]
    operands = (samples, targets.reshape(rows // 128, 128), counts, bucket_ids, sign_bits)
    gram, zty = fused_call(rows)(
        *[pltpu.with_memory_space_constraint(value, pltpu.HBM) for value in operands])
    return gram, zty.reshape(256)


def solution(mesh):
    placed = (P("dp", None), P("dp"), P(), P(), P())
    return jax.shard_map(
        body, mesh=mesh, in_specs=placed, out_specs=(P("dp", "feat"), P("feat")), check_vma=False
    )
```
